256 devices in a mesh: space: 64 (over x, z, core), col: 4 (over y).
Axes of the slice: x: 4, y: 4, z: 8, core: 2. Of those that a mesh axis runs over, the one named last changes fastest.
Arguments:
- snapshots: float32 [262144, 256], P('space', 'col'), may hold values from -80 to 80
- samples: bfloat16 [262144, 4096], P('space', 'col'), may hold values from -6 to 6
- sample_rates: float32 [4096, 8], replicated, may hold values from -4 to 4
- sample_order: int32 [4096], P('col'), may hold values from 0 to 4095, each once
- term_powers: int32 [495, 8], replicated, may hold values from 0 to 4, as said below
Outputs:
- pod_modes: float32 [262144, 64], P('space', 'col')
- mode_coeffs: float32 [4096, 64], P('col')
- fitted: float32 [4096, 64], P('col')
- chaos_coeffs: float32 [495, 64], replicated
The draws below stay inside these ranges and needn't reach their ends.
Inputs may be any that keep to these rules, and one draw needn't show every extreme that they name: `term_powers`: the rows are all multi-indices whose entries sum to at most 4, each exactly once, in an order drawn from the seed.
All inputs are finite; a program needn't handle non-finite values.
Results may differ from the reference program's by a relative error of at most 0.003.
Values sent between devices are 32-bit elements; how exact they have to be, the bound alone decides.
A program may use at most 192 MiB of HBM per device.

```python
import math
import jax
import jax.numpy as jnp
import numpy as np
from jax import lax

M = 256
K = 64
RATES = 8
TERMS = 495
NSAMP = 4096
SWEEPS = 3
R_DEV = 4096
NCELL = 262144
N_SPACE = 64


top_degree = 4


def multi_indices(rate_count, degree_limit):
    table_rows = [[]]
    for position in range(rate_count):
        grown_rows = []
        for current in table_rows:
            degree_used = sum(current)
            for exponent in range(degree_limit - degree_used + 1):
                grown_rows.append(current + [exponent])
        table_rows = grown_rows
    return np.array(table_rows, dtype=np.int32)


def draw_term_powers(key, part):
    candidates = multi_indices(RATES, top_degree)
    order_key = jax.random.fold_in(key, 11)
    picked = jax.random.permutation(order_key, candidates.shape[0]).astype(jnp.int32)
    return jnp.asarray(candidates)[picked[:TERMS]]


def draw_snapshots(key, part):
    noise_key = jax.random.fold_in(key, 21)
    row_key = jax.random.fold_in(key, 22)
    col_key = jax.random.fold_in(key, 23)
    noise_values = jax.random.truncated_normal(noise_key, -4.0, 4.0, (NCELL, M), jnp.float32)
    row_scale = jnp.exp(jax.random.uniform(row_key, (NCELL,), jnp.float32, 0.0, math.log(10.0)))
    col_scale = jnp.exp(jax.random.uniform(col_key, (M,), jnp.float32, math.log(0.5), math.log(2.0)))
    return noise_values * row_scale[:, None] * col_scale[None, :]


def shard_levels(key, dims, shards, least, high):
    def one(axis_at, parts):
        draws = jax.random.uniform(jax.random.fold_in(jax.random.fold_in(key, 6), axis_at), (parts,), jnp.float32, least / len(shards), high / len(shards))
        return jnp.repeat(jnp.exp(draws), dims[axis_at] // parts).reshape((-1,) + (1,) * (len(dims) - axis_at - 1))

    factor_of = one(*shards[0])
    for cut in shards[1:]:
        factor_of = factor_of * one(*cut)
    return factor_of


def noise(rng, extent, spread, bound, pieces=(), kind=jnp.bfloat16):
    gain = shard_levels(rng, extent, pieces, -0.22, 0.18) if pieces else 1.0
    result = jax.random.normal(rng, extent, jnp.float32) * spread * gain
    return jnp.minimum(jnp.maximum(result, -bound), bound).astype(kind)


def setup_inputs(seed: int = 0) -> dict:
    arg_keys = jax.random.split(jax.random.key(seed), 6)
    return {
        "snapshots": draw_snapshots(jax.random.fold_in(arg_keys[5], 71), 0),
        "samples": noise(arg_keys[1], (NCELL, NSAMP), 1.0, 6.0, ((0, 64), (1, 4))),
        "sample_rates": noise(arg_keys[2], (NSAMP, RATES), 1.0, 4.0, (), jnp.float32),
        "sample_order": jax.random.permutation(arg_keys[3], NSAMP).astype(jnp.int32),
        "term_powers": draw_term_powers(jax.random.fold_in(arg_keys[5], 71), 0),
    }


top_degree = 4
ridge = 0.05

def contract(left, right):
    return lax.dot_general(left.astype(jnp.float32), right.astype(jnp.float32), (((0,), (0,)), ((), ())), precision=lax.Precision.HIGHEST, preferred_element_type=jnp.float32)

def orthonormal_basis(snapshot_gram, modes_count):
    lower_factor = jnp.linalg.cholesky(snapshot_gram)
    reduced = jnp.dot(lower_factor.T, lower_factor, precision=lax.Precision.HIGHEST)
    subspace = jnp.eye(snapshot_gram.shape[0], modes_count, dtype=jnp.float32)
    for sweep_index in range(SWEEPS):
        images = jnp.dot(reduced, subspace, precision=lax.Precision.HIGHEST)
        factor = jnp.linalg.cholesky(contract(images, images))
        subspace = lax.linalg.triangular_solve(factor, images, left_side=False, lower=True, transpose_a=True)
    return lax.linalg.triangular_solve(lower_factor, subspace, left_side=True, lower=True, transpose_a=True)

def hermite_features(points, term_powers):
    levels = [jnp.ones_like(points), points]
    for degree_index in range(1, top_degree):
        levels.append(points * levels[degree_index] - degree_index * levels[degree_index - 1])
    scaled = [levels[degree_index] / math.sqrt(math.factorial(degree_index)) for degree_index in range(top_degree + 1)]
    hermite_table = jnp.stack(scaled, axis=-1)
    selector = (term_powers[:, :, None] == jnp.arange(top_degree + 1, dtype=jnp.int32)[None, None, :]).astype(points.dtype)
    features = jnp.ones((points.shape[0], term_powers.shape[0]), points.dtype)
    for rate_index in range(term_powers.shape[1]):
        features = features * jnp.dot(hermite_table[:, rate_index, :], selector[:, rate_index, :].T, precision=lax.Precision.HIGHEST)
    return features

def solve_system(features, right_hand, sample_count):
    system = contract(features, features) + ridge * sample_count * jnp.eye(features.shape[1], dtype=jnp.float32)
    factor = jnp.linalg.cholesky(system)
    middle = lax.linalg.triangular_solve(factor, right_hand, left_side=True, lower=True, transpose_a=False)
    return lax.linalg.triangular_solve(factor, middle, left_side=True, lower=True, transpose_a=True)

def reference(snapshots, samples, sample_rates, sample_order, term_powers):
    snapshot_gram = contract(snapshots, snapshots)
    projector = orthonormal_basis(snapshot_gram, K)
    mode_rows = jnp.dot(snapshots, projector, precision=lax.Precision.HIGHEST)
    pod_modes = math.sqrt(NCELL) * mode_rows
    mode_low = mode_rows.astype(jnp.bfloat16).reshape(N_SPACE, R_DEV, K)
    sample_blocks = samples.reshape(N_SPACE, R_DEV, NSAMP)

    def accumulate(carry, pair):
        return (carry + lax.dot_general(pair[1].astype(jnp.float32), pair[0].astype(jnp.float32), (((0,), (0,)), ((), ())), preferred_element_type=jnp.float32), None)
    mode_coeffs, ignored = lax.scan(accumulate, jnp.zeros((NSAMP, K), jnp.float32), (mode_low, sample_blocks))
    features = hermite_features(sample_rates[sample_order], term_powers)
    right_hand = contract(features, mode_coeffs)
    surrogate = solve_system(features, right_hand, NSAMP)
    fitted = jnp.dot(features, surrogate, precision=lax.Precision.HIGHEST)
    chaos_coeffs = math.sqrt(NSAMP) * surrogate
    return (pod_modes, mode_coeffs, fitted, chaos_coeffs)
```

```python
import functools
import itertools
import math

import jax
import jax.numpy as jnp
import numpy as np
from jax import lax
from jax.experimental import pallas as pl
from jax.experimental.pallas import tpu as pltpu
from jax.sharding import PartitionSpec as P

K = 64
M = 256
SWEEPS = 3
NX, NZ, NY = 4, 8, 4

top_degree = 4
ridge = 0.05

EXACT = lax.Precision.HIGHEST
TERM_PAD = 512
TABLE = 256
PART = 80
CHUNK = 512
BLOCK = 128
MESH = pl.DeviceIdType.MESH
VMEM = pl.BlockSpec(memory_space=pltpu.VMEM)


def nn(a, b, precision=EXACT):
    return lax.dot_general(
        a, b, (((1,), (0,)), ((), ())), precision=precision, preferred_element_type=jnp.float32
    )


def nt(a, b, precision=EXACT):
    return lax.dot_general(
        a, b, (((1,), (1,)), ((), ())), precision=precision, preferred_element_type=jnp.float32
    )


def tn(a, b, precision=EXACT):
    return lax.dot_general(
        a, b, (((0,), (0,)), ((), ())), precision=precision, preferred_element_type=jnp.float32
    )


def cost(flops, bytes_accessed):
    return pl.CostEstimate(flops=flops, bytes_accessed=bytes_accessed, transcendentals=0)


def eye(n):
    rows = lax.broadcasted_iota(jnp.int32, (n, n), 0)
    return (rows == lax.broadcasted_iota(jnp.int32, (n, n), 1)).astype(jnp.float32)


def inverse_factor(aug, out, n):
    w = 2 * n
    groups = n // 8
    sub = lax.broadcasted_iota(jnp.int32, (8, w), 0)

    def body(b, carry):
        top = aug[0:8, :]
        r = [jnp.broadcast_to(top[k : k + 1, :], (8, w)) for k in range(8)]
        a = [[jnp.broadcast_to(r[i][:, j : j + 1], (8, w)) for j in range(i + 1)] for i in range(8)]
        low = [[None] * 8 for _ in range(8)]
        inv = [None] * 8
        for j in range(8):
            inv[j] = 1.0 / a[j][j]
            for i in range(j + 1, 8):
                low[i][j] = a[i][j] * inv[j]
            for i in range(j + 1, 8):
                for k in range(j + 1, i + 1):
                    a[i][k] = a[i][k] - low[i][j] * a[k][j]
                r[i] = r[i] - low[i][j] * r[j]
        q = [None] * 8
        for k in reversed(range(8)):
            v = r[k] * inv[k]
            for m in reversed(range(k + 1, 8)):
                v = v - low[m][k] * q[m]
            q[k] = v
        rows = r[0] * lax.rsqrt(a[0][0])
        for k in range(1, 8):
            rows = jnp.where(sub == k, r[k] * lax.rsqrt(a[k][k]), rows)
        out[pl.ds(pl.multiple_of(8 * b, 8), 8), :] = pltpu.roll(rows, 8 * b + n, 1)[:, :n]
        rest = aug[8:n, :].reshape(groups - 1, 8, w)
        upd = rest
        for k in range(8):
            upd = upd - jnp.broadcast_to(rest[:, :, k : k + 1], rest.shape) * q[k][None]
        aug[0 : n - 8, :] = pltpu.roll(upd.reshape(n - 8, w), w - 8, 1)
        return carry

    lax.fori_loop(0, groups, body, 0)


def pod_kernel(g_ref, p_ref, aug, cinv):
    def factor(m):
        aug[...] = jnp.concatenate([m, eye(K)], axis=1)
        inverse_factor(aug, cinv, K)
        return cinv[...]

    z = nn(factor(g_ref[0:K, 0:K]), g_ref[0:K, :])
    for sweep in range(SWEEPS):
        w = nn(z, g_ref[...])
        c = factor(nt(z, w))
        z = nn(c, w if sweep < SWEEPS - 1 else z)
    p_ref[...] = z


def projector_rows(gram):
    return pl.pallas_call(
        pod_kernel,
        out_shape=jax.ShapeDtypeStruct((K, M), jnp.float32),
        in_specs=[VMEM],
        out_specs=VMEM,
        scratch_shapes=[pltpu.VMEM((K, 2 * K), jnp.float32), pltpu.VMEM((K, K), jnp.float32)],
        cost_estimate=cost(10**9, 10**6),
    )(gram)


def combos():
    return [c for c in itertools.product(range(top_degree + 1), repeat=4) if sum(c) <= top_degree]


def selectors(powers_t):
    row = np.full((TABLE,), -1, np.int32)
    for m, c in enumerate(combos()):
        for part in range(3):
            row[PART * part + m] = sum(e * 5**i for i, e in enumerate(c))
    weights = jnp.asarray(np.array([[1], [5], [25], [125]], np.int32))

    def one(powers):
        code = jnp.sum(powers * weights, axis=0)
        code = jnp.pad(code, (0, TERM_PAD - code.shape[0]), constant_values=-7)
        return (code[:, None] == jnp.asarray(row)[None, :]).astype(jnp.bfloat16)

    return one(powers_t[:4]), one(powers_t[4:])


def fill_table(levels, first, parts, table):
    for m, c in enumerate(combos()):
        row = None
        for i, e in enumerate(c):
            if e:
                level = levels[e][first + i : first + i + 1, :]
                row = level if row is None else row * level
        table[m : m + 1, :] = jnp.ones_like(levels[1][0:1, :]) if row is None else row
    full = table[...]
    high = full.astype(jnp.bfloat16)
    left = full - high.astype(jnp.float32)
    mid = left.astype(jnp.bfloat16)
    parts[0:PART, :] = high
    parts[PART : 2 * PART, :] = mid
    parts[2 * PART : 3 * PART, :] = (left - mid.astype(jnp.float32)).astype(jnp.bfloat16)


def feature_kernel(total, rates_ref, sa_ref, sb_ref, sys_ref, f_ref, hh, hl, ta, tb, table):
    step = pl.program_id(0)

    @pl.when(step == 0)
    def _():
        for ref in (hh, hl, ta, tb, table):
            ref[...] = jnp.zeros_like(ref)

    v = rates_ref[...]
    he = [jnp.ones_like(v), v]
    for d in range(1, top_degree):
        he.append(v * he[d] - d * he[d - 1])
    levels = [he[d] / math.sqrt(math.factorial(d)) for d in range(top_degree + 1)]
    fill_table(levels, 0, ta, table)
    fill_table(levels, 4, tb, table)
    f = nn(sa_ref[...], ta[...], None) * nn(sb_ref[...], tb[...], None)
    f_ref[...] = f

    @pl.when(step < total // CHUNK)
    def _():
        high = f.astype(jnp.bfloat16)
        low = (f - high.astype(jnp.float32)).astype(jnp.bfloat16)
        hh[...] += nt(high, high, None)
        hl[...] += nt(high, low, None)

    @pl.when(step == pl.num_programs(0) - 1)
    def _():
        sys_ref[...] = hh[...] + hl[...] + hl[...].T + (ridge * total) * eye(TERM_PAD)


def features_and_system(rates_t, pick_a, pick_b, total):
    cols = rates_t.shape[1]
    first = total // CHUNK
    square = pltpu.VMEM((TERM_PAD, TERM_PAD), jnp.float32)
    parts = pltpu.VMEM((TABLE, CHUNK), jnp.bfloat16)
    whole = lambda i: (0, 0)
    return pl.pallas_call(
        functools.partial(feature_kernel, total),
        grid=(cols // CHUNK,),
        out_shape=(
            jax.ShapeDtypeStruct((TERM_PAD, TERM_PAD), jnp.float32),
            jax.ShapeDtypeStruct((TERM_PAD, cols - total), jnp.float32),
        ),
        in_specs=[
            pl.BlockSpec((8, CHUNK), lambda i: (0, i)),
            pl.BlockSpec((TERM_PAD, TABLE), whole),
            pl.BlockSpec((TERM_PAD, TABLE), whole),
        ],
        out_specs=(
            pl.BlockSpec((TERM_PAD, TERM_PAD), whole),
            pl.BlockSpec((TERM_PAD, CHUNK), lambda i: (0, jnp.maximum(i - first, 0))),
        ),
        scratch_shapes=[square, square, parts, parts, pltpu.VMEM((PART, CHUNK), jnp.float32)],
        cost_estimate=cost(2 * 10**10, 4 * 10**6),
    )(rates_t, pick_a, pick_b)


def invert_kernel(sys_ref, out_ref, aug, linv, amat, ymat):
    amat[...] = sys_ref[...]
    ymat[...] = jnp.zeros_like(ymat)
    for lo in range(0, TERM_PAD, BLOCK):
        hi = lo + BLOCK
        aug[...] = jnp.concatenate([amat[lo:hi, lo:hi], eye(BLOCK)], axis=1)
        inverse_factor(aug, linv, BLOCK)
        li = linv[...]
        if lo:
            ymat[lo:hi, 0:lo] = nn(li, ymat[lo:hi, 0:lo])
        ymat[lo:hi, lo:hi] = li
        if hi < TERM_PAD:
            panel = nt(amat[hi:, lo:hi], li)
            amat[hi:, hi:] = amat[hi:, hi:] - nt(panel, panel)
            ymat[hi:, 0:hi] = ymat[hi:, 0:hi] - nn(panel, ymat[lo:hi, 0:hi])
    out_ref[...] = tn(ymat[...], ymat[...])


def inverse(system):
    square = pltpu.VMEM((TERM_PAD, TERM_PAD), jnp.float32)
    return pl.pallas_call(
        invert_kernel,
        out_shape=jax.ShapeDtypeStruct((TERM_PAD, TERM_PAD), jnp.float32),
        in_specs=[VMEM],
        out_specs=VMEM,
        scratch_shapes=[
            pltpu.VMEM((BLOCK, 2 * BLOCK), jnp.float32),
            pltpu.VMEM((BLOCK, BLOCK), jnp.float32),
            square,
            square,
        ],
        cost_estimate=cost(3 * 10**10, 3 * 10**6),
    )(system)


def split(x):
    high = x.astype(jnp.bfloat16)
    return high, (x - high.astype(jnp.float32)).astype(jnp.bfloat16)


def partial_kernel(y_ref, s0, s1, s2, s3, samples_ref, w_ref, g_ref, acc, gacc):
    step = pl.program_id(0)
    y = y_ref[0]

    pieces = [split(s[...]) for s in (s0, s1, s2, s3)]
    both = jnp.concatenate([p[0] for p in pieces] + [p[1] for p in pieces], axis=0)
    acc[...] = jnp.where(step > 0, acc[...], 0.0) + nn(both, samples_ref[...], None)
    gacc[...] = jnp.where(step > 0, gacc[...], 0.0) + nt(
        jnp.concatenate(pieces[0], axis=0), both, None
    )

    @pl.when(step == pl.num_programs(0) - 1)
    def _():
        for d in range(NY):
            at = pl.multiple_of(lax.rem(y + d, NY) * K, K)
            lo = K * d
            w_ref[pl.ds(at, K), :] = acc[lo : lo + K, :] + acc[M + lo : M + lo + K, :]
        g = (gacc[0:K, 0:M] + gacc[0:K, M:]) + (gacc[K:, 0:M] + gacc[K:, M:])
        g_ref[...] = pltpu.roll(g, y * K, 1)


def partial_sums(shards, samples):
    rows, width = samples.shape
    chunk = 512
    shard = pl.BlockSpec((K, chunk), lambda i: (0, i))
    return pl.pallas_call(
        partial_kernel,
        grid=(rows // chunk,),
        out_shape=(
            jax.ShapeDtypeStruct((M, width), jnp.float32),
            jax.ShapeDtypeStruct((K, M), jnp.float32),
        ),
        in_specs=[pl.BlockSpec(memory_space=pltpu.SMEM)]
        + [shard] * NY
        + [pl.BlockSpec((chunk, width), lambda i: (i, 0))],
        out_specs=(
            pl.BlockSpec((M, width), lambda i: (0, 0)),
            pl.BlockSpec((K, M), lambda i: (0, 0)),
        ),
        scratch_shapes=[
            pltpu.VMEM((2 * M, width), jnp.float32),
            pltpu.VMEM((2 * K, 2 * M), jnp.float32),
        ],
        cost_estimate=cost(5 * 10**9, 14 * 10**6),
    )(lax.axis_index("col").astype(jnp.int32)[None], *shards, samples)


def place():
    s = lax.axis_index("space")
    return s // (NZ * 2), (s // 2) % NZ, s % 2, lax.axis_index("col")


def device(x, z, c, y):
    return {"space": (x * NZ + z) * 2 + c, "col": y}


def greet(peers):
    barrier = pltpu.get_barrier_semaphore()
    for peer in peers:
        pl.semaphore_signal(barrier, inc=1, device_id=peer, device_id_type=MESH)
    pl.semaphore_wait(barrier, len(peers))


def send(src, dst, send_sem, recv_sem, peer):
    copy = pltpu.make_async_remote_copy(
        src_ref=src,
        dst_ref=dst,
        send_sem=send_sem,
        recv_sem=recv_sem,
        device_id=peer,
        device_id_type=MESH,
    )
    copy.start()
    return copy


def lanes(k):
    return pl.ds(pl.multiple_of(k * 128, 128), 128)


def reduce_kernel(
    w_ref, g_ref, w_out, g_out,
    cw, cg, sxw, sxg, rxw, rxg, xw, zw, zg, wfull, gx, gfull,
    s_c, r_c, s_x, r_x, s_z, r_z, s_wz, r_wz, s_gx, r_gx, s_gy, r_gy, s_gc, r_gc,
):
    x, z, c, y = place()
    xs = [lax.rem(x + d, NX) for d in range(NX)]
    zs = [lax.rem(z + d, NZ) for d in range(NZ)]
    ys = [lax.rem(y + d, NY) for d in range(NY)]
    partner = device(x, z, 1 - c, y)
    x_peers = [device(xs[d], z, c, y) for d in range(NX)]
    z_peers = [device(x, zs[d], c, y) for d in range(NZ)]
    y_peers = [device(x, z, c, ys[d]) for d in range(NY)]
    x_order, z_order, y_order = (2, 1, 3, 0), (4, 3, 5, 2, 6, 1, 7), (2, 1, 3)
    greet([partner] + x_peers[1:] + z_peers[1:] + y_peers[1:])
    sent = []

    first = {}
    for d in x_order:
        other = (1 - c) * NX + xs[d]
        rows = pl.ds(pl.multiple_of(other * 8, 8), 8)
        first[d] = (
            send(g_ref.at[rows, :], cg.at[d], s_c.at[0, d], r_c.at[0, d], partner),
            send(w_ref.at[:, lanes(other)], cw.at[d], s_c.at[1, d], r_c.at[1, d], partner),
        )
        sent += first[d]
    second = {}
    for d in x_order:
        mine = c * NX + xs[d]
        for copy in first[d]:
            copy.wait_recv()
        gsum = g_ref[pl.ds(pl.multiple_of(mine * 8, 8), 8), :] + cg[d]
        wsum = w_ref[:, lanes(mine)] + cw[d]
        if d:
            sxg[d] = gsum
            sxw[d] = wsum
            second[d] = (
                send(sxg.at[d], rxg.at[x], s_x.at[0, d], r_x.at[0, d], x_peers[d]),
                send(sxw.at[d], rxw.at[x], s_x.at[1, d], r_x.at[1, d], x_peers[d]),
            )
            sent += second[d]
        else:
            rxg[pl.ds(x, 1)] = gsum[None]
            rxw[pl.ds(x, 1)] = wsum[None]
    for d in (1, 3, 2):
        second[d][0].wait_recv()
    sxg[0] = ((rxg[0] + rxg[1]) + rxg[2]) + rxg[3]
    zg[pl.ds(z, 1)] = sxg[0][None]
    third = {}
    for d in z_order:
        third[d] = [send(sxg.at[0], zg.at[z], s_z.at[0, d], r_z.at[0, d], z_peers[d])]
    for d in (1, 3, 2):
        second[d][1].wait_recv()
    xw[...] = (((rxw[0] + rxw[1]) + rxw[2]) + rxw[3]).reshape(xw.shape)
    for d in z_order:
        third[d].append(send(xw.at[zs[d]], zw.at[z], s_z.at[1, d], r_z.at[1, d], z_peers[d]))
        sent += third[d]
    zw[pl.ds(z, 1)] = xw[pl.ds(z, 1)]

    for d in z_order:
        third[d][0].wait_recv()
    total = zg[0]
    for k in range(1, NZ):
        total = total + zg[k]
    gx[pl.ds(x, 1)] = total[None]
    fourth = {}
    for d in (2, 1, 3):
        fourth[d] = send(gx.at[x], gx.at[x], s_gx.at[d], r_gx.at[d], x_peers[d])
        sent.append(fourth[d])

    for d in z_order:
        third[d][1].wait_recv()
    total = zw[0]
    for k in range(1, NZ):
        total = total + zw[k]
    wfull[pl.ds(z, 1)] = total[None]
    fifth = {}
    for d in z_order:
        fifth[d] = send(wfull.at[z], wfull.at[z], s_wz.at[d], r_wz.at[d], z_peers[d])
        sent.append(fifth[d])

    for d in (1, 3, 2):
        fourth[d].wait_recv()
    gfull[pl.ds(y, 1), pl.ds(c, 1)] = gx[...][None, None]
    sixth = {}
    for d in y_order:
        sixth[d] = send(gx, gfull.at[y, c], s_gy.at[d], r_gy.at[d], y_peers[d])
        sent.append(sixth[d])
    seventh = [send(gx, gfull.at[y, c], s_gc.at[0], r_gc.at[0], partner)]
    for d in (1, 3, 2):
        sixth[d].wait_recv()
        src = lax.rem(y + NY - d, NY)
        seventh.append(send(gfull.at[src, c], gfull.at[src, c], s_gc.at[d], r_gc.at[d], partner))
    sent += seventh
    for copy in seventh:
        copy.wait_recv()
    for k in range(NY):
        g_out[K * k : K * k + K, :] = gfull[k].reshape(K, M)
    for d in z_order:
        fifth[d].wait_recv()
    w_out[...] = wfull[...].reshape(M, 128)
    for copy in sent:
        copy.wait_send()


def reduce_over_space(w, g):
    f32 = jnp.float32
    dma = pltpu.SemaphoreType.DMA
    return pl.pallas_call(
        reduce_kernel,
        out_shape=(jax.ShapeDtypeStruct((M, 128), f32), jax.ShapeDtypeStruct((M, M), f32)),
        in_specs=[VMEM, VMEM],
        out_specs=(VMEM, VMEM),
        scratch_shapes=[
            pltpu.VMEM((NX, M, 128), f32),
            pltpu.VMEM((NX, 8, M), f32),
            pltpu.VMEM((NX, M, 128), f32),
            pltpu.VMEM((NX, 8, M), f32),
            pltpu.VMEM((NX, M, 128), f32),
            pltpu.VMEM((NX, 8, M), f32),
            pltpu.VMEM((NZ, M // NZ, 128), f32),
            pltpu.VMEM((NZ, M // NZ, 128), f32),
            pltpu.VMEM((NZ, 8, M), f32),
            pltpu.VMEM((NZ, M // NZ, 128), f32),
            pltpu.VMEM((NX, 8, M), f32),
            pltpu.VMEM((NY, 2, NX, 8, M), f32),
            dma((2, NX)), dma((2, NX)),
            dma((2, NX)), dma((2, NX)),
            dma((2, NZ)), dma((2, NZ)),
            dma((NZ,)), dma((NZ,)),
            dma((NX,)), dma((NX,)),
            dma((NY,)), dma((NY,)),
            dma((NY,)), dma((NY,)),
        ],
        compiler_params=pltpu.CompilerParams(collective_id=0, has_side_effects=True),
        cost_estimate=cost(10**7, 3 * 10**6),
    )(w, g)


def finish_kernel(
    p_ref, w_ref, f_ref, sinv_ref, mc_out, fit_out, chaos_out,
    mall, half, ry, rfull,
    s_x, r_x, s_c, r_c, s_y, r_y, s_p, r_p,
):
    x, z, c, y = place()
    xs = [lax.rem(x + d, NX) for d in range(NX)]
    ys = [lax.rem(y + d, NY) for d in range(NY)]
    partner = device(x, z, 1 - c, y)
    x_peers = [device(xs[d], z, c, y) for d in range(NX)]
    y_peers = [device(x, z, c, ys[d]) for d in range(NY)]
    greet([partner] + x_peers[1:] + y_peers[1:])
    sent = []
    mine = mall.at[c, x]
    mall[pl.ds(c, 1), pl.ds(x, 1)] = nn(p_ref[...], w_ref[...])[None, None]
    swaps = [send(mine, mine, s_c.at[0], r_c.at[0], partner)]
    moves = {}
    for d in (2, 1, 3):
        moves[d] = send(mine, mine, s_x.at[d], r_x.at[d], x_peers[d])
    for d in (1, 3, 2):
        moves[d].wait_recv()
        src = mall.at[c, lax.rem(x + NX - d, NX)]
        swaps.append(send(src, src, s_c.at[d], r_c.at[d], partner))
    for copy in swaps:
        copy.wait_recv()
    sent += swaps + list(moves.values())
    coeffs = jnp.concatenate([mall[k // NX, k % NX] for k in range(2 * NX)], axis=1)
    mc_out[...] = coeffs
    part = nt(coeffs, f_ref[...])
    half[...] = jnp.concatenate([part[:, 0:256], part[:, 256:]], axis=0).reshape(half.shape)
    rows = half.at[c]
    ry[pl.ds(y, 1)] = half[pl.ds(c, 1)]
    trade = {}
    for d in (2, 1, 3):
        trade[d] = send(rows, ry.at[y], s_y.at[d], r_y.at[d], y_peers[d])
    for d in (1, 3, 2):
        trade[d].wait_recv()
    rfull[pl.ds(c, 1)] = (((ry[0] + ry[1]) + ry[2]) + ry[3])[None]
    last = send(rfull.at[c], rfull.at[c], s_p.at[0], r_p.at[0], partner)
    last.wait_recv()
    sent += list(trade.values()) + [last]
    right = jnp.concatenate([rfull[0], rfull[1]], axis=1)
    surrogate = nn(right, sinv_ref[...])
    fit_out[...] = nn(surrogate, f_ref[...])
    chaos_out[...] = surrogate
    for copy in sent:
        copy.wait_send()


def finish(p_rows, w_block, f_local, sys_inverse):
    f32 = jnp.float32
    dma = pltpu.SemaphoreType.DMA
    width = f_local.shape[1]
    return pl.pallas_call(
        finish_kernel,
        out_shape=(
            jax.ShapeDtypeStruct((K, width), f32),
            jax.ShapeDtypeStruct((K, width), f32),
            jax.ShapeDtypeStruct((K, TERM_PAD), f32),
        ),
        in_specs=[VMEM] * 4,
        out_specs=(VMEM,) * 3,
        scratch_shapes=[
            pltpu.VMEM((2, NX, K, 128), f32),
            pltpu.VMEM((2, K, 256), f32),
            pltpu.VMEM((NY, K, 256), f32),
            pltpu.VMEM((2, K, 256), f32),
            dma((NX,)), dma((NX,)),
            dma((NX,)), dma((NX,)),
            dma((NY,)), dma((NY,)),
            dma((1,)), dma((1,)),
        ],
        compiler_params=pltpu.CompilerParams(collective_id=1, has_side_effects=True),
        cost_estimate=cost(10**9, 6 * 10**6),
    )(p_rows, w_block, f_local, sys_inverse)


def modes_kernel(p_ref, s0, s1, s2, s3, out_ref):
    total = nn(p_ref[0], s0[...])
    for d, s in enumerate((s1, s2, s3)):
        total = total + nn(p_ref[d + 1], s[...])
    out_ref[...] = total


def modes(p_slices, shards):
    cells = shards[0].shape[1]
    chunk = 1024
    width = p_slices.shape[1]
    shard = pl.BlockSpec((K, chunk), lambda i: (0, i))
    return pl.pallas_call(
        modes_kernel,
        grid=(cells // chunk,),
        out_shape=jax.ShapeDtypeStruct((width, cells), jnp.float32),
        in_specs=[pl.BlockSpec((NY, width, K), lambda i: (0, 0, 0))] + [shard] * NY,
        out_specs=pl.BlockSpec((width, chunk), lambda i: (0, i)),
        cost_estimate=cost(10**8, 5 * 10**6),
    )(p_slices, *shards)


def local(snapshots, samples, sample_rates, sample_order, term_powers):
    y = lax.axis_index("col")
    own = snapshots.T
    up = [(i, (i + 1) % NY) for i in range(NY)]
    down = [(i, (i + NY - 1) % NY) for i in range(NY)]
    after = lax.ppermute(own, "col", down)
    before = lax.ppermute(own, "col", up)
    far = jnp.concatenate(
        [lax.ppermute(after[: K // 2], "col", down), lax.ppermute(before[K // 2 :], "col", up)], axis=0
    )
    shards = (own, after, far, before)

    total = sample_rates.shape[0]
    terms = term_powers.shape[0]
    rates_t = jnp.concatenate([sample_rates.T, sample_rates[sample_order].T], axis=1)
    pick_a, pick_b = selectors(term_powers.T)
    system, f_local = features_and_system(rates_t, pick_a, pick_b, total)
    sys_inverse = inverse(system)

    w_part, g_part = partial_sums(shards, samples)
    w_block, gram = reduce_over_space(w_part, g_part)
    p_rows = projector_rows(gram)

    cell_count = snapshots.shape[0] * lax.axis_size("space")
    width = K // NY
    slices = lax.dynamic_slice_in_dim(p_rows, y * width, width, 0) * math.sqrt(cell_count)
    slices = jnp.roll(slices.reshape(width, NY, K).transpose(1, 0, 2), -y, axis=0)
    pod_modes = modes(slices, shards).T
    coeffs, fitted, surrogate = finish(p_rows, w_block, f_local, sys_inverse)
    chaos_coeffs = math.sqrt(total) * surrogate[:, :terms].T
    return (pod_modes, coeffs.T, fitted.T, chaos_coeffs)


def solution(mesh):
    placed = (P("space", "col"), P("space", "col"), P(), P("col"), P())
    return jax.shard_map(
        local,
        mesh=mesh,
        in_specs=placed,
        out_specs=(P("space", "col"), P("col", None), P("col", None), P()),
        check_vma=False,
    )
```

```python
import functools
import itertools
import math

import jax
import jax.numpy as jnp
import numpy as np
from jax import lax
from jax.experimental import pallas as pl
from jax.experimental.pallas import tpu as pltpu
from jax.sharding import PartitionSpec as P

K = 64
M = 256
SWEEPS = 3
NX, NZ, NY = 4, 8, 4

top_degree = 4
ridge = 0.05

EXACT = lax.Precision.HIGHEST
TERM_PAD = 512
TABLE = 256
PART = 80
CHUNK = 1024
BLOCK = 128
MESH = pl.DeviceIdType.MESH
VMEM = pl.BlockSpec(memory_space=pltpu.VMEM)


def nn(a, b, precision=EXACT):
    return lax.dot_general(
        a, b, (((1,), (0,)), ((), ())), precision=precision, preferred_element_type=jnp.float32
    )


def nt(a, b, precision=EXACT):
    return lax.dot_general(
        a, b, (((1,), (1,)), ((), ())), precision=precision, preferred_element_type=jnp.float32
    )


def tn(a, b, precision=EXACT):
    return lax.dot_general(
        a, b, (((0,), (0,)), ((), ())), precision=precision, preferred_element_type=jnp.float32
    )


def cost(flops, bytes_accessed):
    return pl.CostEstimate(flops=flops, bytes_accessed=bytes_accessed, transcendentals=0)


def eye(n):
    rows = lax.broadcasted_iota(jnp.int32, (n, n), 0)
    return (rows == lax.broadcasted_iota(jnp.int32, (n, n), 1)).astype(jnp.float32)


def inverse_factor(aug, out, n):
    w = 2 * n
    groups = n // 8
    sub = lax.broadcasted_iota(jnp.int32, (8, w), 0)

    def body(b, carry):
        top = aug[0:8, :]
        r = [jnp.broadcast_to(top[k : k + 1, :], (8, w)) for k in range(8)]
        a = [[jnp.broadcast_to(r[i][:, j : j + 1], (8, w)) for j in range(i + 1)] for i in range(8)]
        low = [[None] * 8 for _ in range(8)]
        inv = [None] * 8
        for j in range(8):
            inv[j] = 1.0 / a[j][j]
            for i in range(j + 1, 8):
                low[i][j] = a[i][j] * inv[j]
            for i in range(j + 1, 8):
                for k in range(j + 1, i + 1):
                    a[i][k] = a[i][k] - low[i][j] * a[k][j]
                r[i] = r[i] - low[i][j] * r[j]
        q = [None] * 8
        for k in reversed(range(8)):
            v = r[k] * inv[k]
            for m in reversed(range(k + 1, 8)):
                v = v - low[m][k] * q[m]
            q[k] = v
        rows = r[0] * lax.rsqrt(a[0][0])
        for k in range(1, 8):
            rows = jnp.where(sub == k, r[k] * lax.rsqrt(a[k][k]), rows)
        out[pl.ds(pl.multiple_of(8 * b, 8), 8), :] = pltpu.roll(rows, 8 * b + n, 1)[:, :n]
        rest = aug[8:n, :].reshape(groups - 1, 8, w)
        upd = rest
        for k in range(8):
            upd = upd - jnp.broadcast_to(rest[:, :, k : k + 1], rest.shape) * q[k][None]
        aug[0 : n - 8, :] = pltpu.roll(upd.reshape(n - 8, w), w - 8, 1)
        return carry

    lax.fori_loop(0, groups, body, 0)


def pod_rows(gram, aug, cinv):
    def factor(m):
        aug[:, 0 : 2 * K] = jnp.concatenate([m, eye(K)], axis=1)
        inverse_factor(aug, cinv, K)
        return cinv[...]

    z = nn(factor(gram[0:K, 0:K]), gram[0:K, :])
    for sweep in range(SWEEPS):
        w = nn(z, gram[...])
        c = factor(nt(z, w))
        z = nn(c, w if sweep < SWEEPS - 1 else z)
    return z


def combos():
    return [c for c in itertools.product(range(top_degree + 1), repeat=4) if sum(c) <= top_degree]


def selectors(powers_t):
    row = np.full((TABLE,), -1, np.int32)
    for m, c in enumerate(combos()):
        for part in range(3):
            row[PART * part + m] = sum(e * 5**i for i, e in enumerate(c))
    weights = jnp.asarray(np.array([[1], [5], [25], [125]], np.int32))

    def one(powers):
        code = jnp.sum(powers * weights, axis=0)
        code = jnp.pad(code, (0, TERM_PAD - code.shape[0]), constant_values=-7)
        return (code[:, None] == jnp.asarray(row)[None, :]).astype(jnp.bfloat16)

    return one(powers_t[:4]), one(powers_t[4:])


def fill_table(levels, first, parts, table):
    for m, c in enumerate(combos()):
        row = None
        for i, e in enumerate(c):
            if e:
                level = levels[e][first + i : first + i + 1, :]
                row = level if row is None else row * level
        table[m : m + 1, :] = jnp.ones_like(levels[1][0:1, :]) if row is None else row
    full = table[...]
    high = full.astype(jnp.bfloat16)
    left = full - high.astype(jnp.float32)
    mid = left.astype(jnp.bfloat16)
    parts[0:PART, :] = high
    parts[PART : 2 * PART, :] = mid
    parts[2 * PART : 3 * PART, :] = (left - mid.astype(jnp.float32)).astype(jnp.bfloat16)


def feature_kernel(total, rates_ref, order_ref, sa_ref, sb_ref, sys_ref, f_ref, hh, hl, ta, tb, table, points):
    step = pl.program_id(0)
    last = pl.num_programs(0) - 1

    @pl.when(step == 0)
    def _():
        for ref in (hh, hl, ta, tb, table):
            ref[...] = jnp.zeros_like(ref)

    @pl.when(step < last)
    def _():
        points[...] = rates_ref[:, pl.ds(pl.multiple_of(step * CHUNK, CHUNK), CHUNK)]

    @pl.when(step == last)
    def _():
        rates = rates_ref[...]
        high = rates.astype(jnp.bfloat16).astype(jnp.float32)
        left = rates - high
        mid = left.astype(jnp.bfloat16).astype(jnp.float32)
        parts = jnp.concatenate([high, mid, left - mid, jnp.zeros_like(left)], axis=0).astype(jnp.bfloat16)
        piece = 512
        row = lax.broadcasted_iota(jnp.int32, (piece, CHUNK), 0)
        found = jnp.zeros((32, CHUNK), jnp.float32)
        for at in range(0, total, piece):
            hit = jnp.where(row == order_ref[...] - at, 1.0, 0.0).astype(jnp.bfloat16)
            found = found + nn(parts[:, at : at + piece], hit, None)
        points[...] = (found[0:8] + found[8:16]) + found[16:24]

    v = points[...]
    he = [jnp.ones_like(v), v]
    for d in range(1, top_degree):
        he.append(v * he[d] - d * he[d - 1])
    levels = [he[d] / math.sqrt(math.factorial(d)) for d in range(top_degree + 1)]
    fill_table(levels, 0, ta, table)
    fill_table(levels, 4, tb, table)
    f = nn(sa_ref[...], ta[...], None) * nn(sb_ref[...], tb[...], None)
    f_ref[...] = f

    @pl.when(step < last)
    def _():
        high = f.astype(jnp.bfloat16)
        low = (f - high.astype(jnp.float32)).astype(jnp.bfloat16)
        hh[...] += nt(high, high, None)
        hl[...] += nt(high, low, None)

    @pl.when(step == last)
    def _():
        sys_ref[...] = hh[...] + hl[...] + hl[...].T + (ridge * total) * eye(TERM_PAD)


def features_and_system(rates_t, order, pick_a, pick_b):
    total = rates_t.shape[1]
    square = pltpu.VMEM((TERM_PAD, TERM_PAD), jnp.float32)
    parts = pltpu.VMEM((TABLE, CHUNK), jnp.bfloat16)
    whole = lambda i: (0, 0)
    return pl.pallas_call(
        functools.partial(feature_kernel, total),
        grid=(total // CHUNK + 1,),
        out_shape=(
            jax.ShapeDtypeStruct((TERM_PAD, TERM_PAD), jnp.float32),
            jax.ShapeDtypeStruct((TERM_PAD, CHUNK), jnp.float32),
        ),
        in_specs=[
            pl.BlockSpec((8, total), whole),
            pl.BlockSpec((1, CHUNK), whole),
            pl.BlockSpec((TERM_PAD, TABLE), whole),
            pl.BlockSpec((TERM_PAD, TABLE), whole),
        ],
        out_specs=(
            pl.BlockSpec((TERM_PAD, TERM_PAD), whole),
            pl.BlockSpec((TERM_PAD, CHUNK), whole),
        ),
        scratch_shapes=[
            square,
            square,
            parts,
            parts,
            pltpu.VMEM((PART, CHUNK), jnp.float32),
            pltpu.VMEM((8, CHUNK), jnp.float32),
        ],
        cost_estimate=cost(2 * 10**10, 4 * 10**6),
    )(rates_t, order, pick_a, pick_b)


def inverse_block(lo, amat, ymat, aug, linv):
    hi = lo + BLOCK
    aug[...] = jnp.concatenate([amat[lo:hi, lo:hi], eye(BLOCK)], axis=1)
    inverse_factor(aug, linv, BLOCK)
    li = linv[...]
    if lo:
        ymat[lo:hi, 0:lo] = nn(li, ymat[lo:hi, 0:lo])
    ymat[lo:hi, lo:hi] = li
    if hi < TERM_PAD:
        panel = nt(amat[hi:, lo:hi], li)
        amat[hi:, hi:] = amat[hi:, hi:] - nt(panel, panel)
        ymat[hi:, 0:hi] = ymat[hi:, 0:hi] - nn(panel, ymat[lo:hi, 0:hi])


def first_block_kernel(sys_ref, amat, ymat, aug, linv):
    amat[...] = sys_ref[...]
    ymat[...] = jnp.zeros_like(ymat)
    inverse_block(0, amat, ymat, aug, linv)


ELIMINATION = [
    pltpu.VMEM((BLOCK, 2 * BLOCK), jnp.float32),
    pltpu.VMEM((BLOCK, BLOCK), jnp.float32),
]


def first_block(system):
    square = jax.ShapeDtypeStruct((TERM_PAD, TERM_PAD), jnp.float32)
    return pl.pallas_call(
        first_block_kernel,
        out_shape=(square, square),
        in_specs=[VMEM],
        out_specs=(VMEM, VMEM),
        scratch_shapes=ELIMINATION,
        cost_estimate=cost(10**10, 3 * 10**6),
    )(system)


def split(x):
    high = x.astype(jnp.bfloat16)
    return high, (x - high.astype(jnp.float32)).astype(jnp.bfloat16)


def partial_kernel(y_ref, s0, s1, s2, s3, samples_ref, w_ref, g_ref, parts_ref, acc, gacc):
    step = pl.program_id(0)
    y = y_ref[0]

    pieces = [split(s[...]) for s in (s0, s1, s2, s3)]
    both = jnp.concatenate([p[0] for p in pieces] + [p[1] for p in pieces], axis=0)
    parts_ref[...] = both
    acc[...] = jnp.where(step > 0, acc[...], 0.0) + nn(both, samples_ref[...], None)
    gacc[...] = jnp.where(step > 0, gacc[...], 0.0) + nt(
        jnp.concatenate(pieces[0], axis=0), both, None
    )

    @pl.when(step == pl.num_programs(0) - 1)
    def _():
        for d in range(NY):
            at = pl.multiple_of(lax.rem(y + d, NY) * K, K)
            lo = K * d
            w_ref[pl.ds(at, K), :] = acc[lo : lo + K, :] + acc[M + lo : M + lo + K, :]
        g = (gacc[0:K, 0:M] + gacc[0:K, M:]) + (gacc[K:, 0:M] + gacc[K:, M:])
        g_ref[...] = pltpu.roll(g, y * K, 1)


def partial_sums(shards, samples):
    rows, width = samples.shape
    chunk = 1024
    shard = pl.BlockSpec((K, chunk), lambda i: (0, i))
    return pl.pallas_call(
        partial_kernel,
        grid=(rows // chunk,),
        out_shape=(
            jax.ShapeDtypeStruct((M, width), jnp.float32),
            jax.ShapeDtypeStruct((K, M), jnp.float32),
            jax.ShapeDtypeStruct((2 * M, rows), jnp.bfloat16),
        ),
        in_specs=[pl.BlockSpec(memory_space=pltpu.SMEM)]
        + [shard] * NY
        + [pl.BlockSpec((chunk, width), lambda i: (i, 0))],
        out_specs=(
            pl.BlockSpec((M, width), lambda i: (0, 0)),
            pl.BlockSpec((K, M), lambda i: (0, 0)),
            pl.BlockSpec((2 * M, chunk), lambda i: (0, i)),
        ),
        scratch_shapes=[
            pltpu.VMEM((2 * M, width), jnp.float32),
            pltpu.VMEM((2 * K, 2 * M), jnp.float32),
        ],
        cost_estimate=cost(5 * 10**9, 14 * 10**6),
    )(lax.axis_index("col").astype(jnp.int32)[None], *shards, samples)


def place():
    s = lax.axis_index("space")
    return s // (NZ * 2), (s // 2) % NZ, s % 2, lax.axis_index("col")


def device(x, z, c, y):
    return {"space": (x * NZ + z) * 2 + c, "col": y}


def greet(peers):
    barrier = pltpu.get_barrier_semaphore()
    for peer in peers:
        pl.semaphore_signal(barrier, inc=1, device_id=peer, device_id_type=MESH)
    pl.semaphore_wait(barrier, len(peers))


def send(src, dst, send_sem, recv_sem, peer):
    copy = pltpu.make_async_remote_copy(
        src_ref=src,
        dst_ref=dst,
        send_sem=send_sem,
        recv_sem=recv_sem,
        device_id=peer,
        device_id_type=MESH,
    )
    copy.start()
    return copy


def lanes(k):
    return pl.ds(pl.multiple_of(k * 128, 128), 128)


def main_kernel(
    scale, chaos_scale,
    w_ref, g_ref, a_in, y_in, f_hbm, parts_hbm,
    mc_out, fit_out, chaos_out, pod_out,
    cw, cg, sxw, sxg, rxw, rxg, xw, zw, zg, wfull, gx, gfull,
    amat, ymat, aug, linv, gram, aug_p, cinv, pbuf, f_ref, parts_ref,
    mall, half, ry, rfull,
    s_c, r_c, s_x, r_x, s_z, r_z, s_wz, r_wz, s_gx, r_gx, s_gy, r_gy, s_gc, r_gc,
    s_swap, r_swap, s_mx, r_mx, s_mc, r_mc, s_y, r_y, s_p, r_p, load,
):
    x, z, c, y = place()
    xs = [lax.rem(x + d, NX) for d in range(NX)]
    zs = [lax.rem(z + d, NZ) for d in range(NZ)]
    ys = [lax.rem(y + d, NY) for d in range(NY)]
    partner = device(x, z, 1 - c, y)
    x_peers = [device(xs[d], z, c, y) for d in range(NX)]
    z_peers = [device(x, zs[d], c, y) for d in range(NZ)]
    y_peers = [device(x, z, c, ys[d]) for d in range(NY)]
    x_order, z_order, y_order = (2, 1, 3, 0), (4, 3, 5, 2, 6, 1, 7), (2, 1, 3)
    loads = [
        pltpu.make_async_copy(f_hbm, f_ref, load.at[0]),
        pltpu.make_async_copy(parts_hbm, parts_ref, load.at[1]),
        pltpu.make_async_copy(a_in, amat, load.at[2]),
        pltpu.make_async_copy(y_in, ymat, load.at[3]),
    ]
    for copy in (loads[2], loads[3], loads[0], loads[1]):
        copy.start()
    greet([partner] + x_peers[1:] + z_peers[1:] + y_peers[1:])
    sent = []

    first = {}
    for d in x_order:
        other = (1 - c) * NX + xs[d]
        rows = pl.ds(pl.multiple_of(other * 8, 8), 8)
        first[d] = (
            send(g_ref.at[rows, :], cg.at[d], s_c.at[0, d], r_c.at[0, d], partner),
            send(w_ref.at[:, lanes(other)], cw.at[d], s_c.at[1, d], r_c.at[1, d], partner),
        )
        sent += first[d]
    second = {}
    for d in x_order:
        mine = c * NX + xs[d]
        for copy in first[d]:
            copy.wait_recv()
        gsum = g_ref[pl.ds(pl.multiple_of(mine * 8, 8), 8), :] + cg[d]
        wsum = w_ref[:, lanes(mine)] + cw[d]
        if d:
            sxg[d] = gsum
            sxw[d] = wsum
            second[d] = (
                send(sxg.at[d], rxg.at[x], s_x.at[0, d], r_x.at[0, d], x_peers[d]),
                send(sxw.at[d], rxw.at[x], s_x.at[1, d], r_x.at[1, d], x_peers[d]),
            )
            sent += second[d]
        else:
            rxg[pl.ds(x, 1)] = gsum[None]
            rxw[pl.ds(x, 1)] = wsum[None]

    loads[2].wait()
    loads[3].wait()
    inverse_block(BLOCK, amat, ymat, aug, linv)

    for d in (1, 3, 2):
        second[d][0].wait_recv()
    sxg[0] = ((rxg[0] + rxg[1]) + rxg[2]) + rxg[3]
    zg[pl.ds(z, 1)] = sxg[0][None]
    third = {}
    for d in z_order:
        third[d] = [send(sxg.at[0], zg.at[z], s_z.at[0, d], r_z.at[0, d], z_peers[d])]
    for d in (1, 3, 2):
        second[d][1].wait_recv()
    xw[...] = (((rxw[0] + rxw[1]) + rxw[2]) + rxw[3]).reshape(xw.shape)
    for d in z_order:
        third[d].append(send(xw.at[zs[d]], zw.at[z], s_z.at[1, d], r_z.at[1, d], z_peers[d]))
        sent += third[d]
    zw[pl.ds(z, 1)] = xw[pl.ds(z, 1)]

    inverse_block(2 * BLOCK, amat, ymat, aug, linv)

    for d in z_order:
        third[d][0].wait_recv()
    total = zg[0]
    for k in range(1, NZ):
        total = total + zg[k]
    gx[pl.ds(x, 1)] = total[None]
    fourth = {}
    for d in (2, 1, 3):
        fourth[d] = send(gx.at[x], gx.at[x], s_gx.at[d], r_gx.at[d], x_peers[d])
        sent.append(fourth[d])

    for d in z_order:
        third[d][1].wait_recv()
    total = zw[0]
    for k in range(1, NZ):
        total = total + zw[k]
    wfull[pl.ds(z, 1)] = total[None]
    fifth = {}
    for d in z_order:
        fifth[d] = send(wfull.at[z], wfull.at[z], s_wz.at[d], r_wz.at[d], z_peers[d])
        sent.append(fifth[d])

    for d in (1, 3, 2):
        fourth[d].wait_recv()
    gfull[pl.ds(y, 1), pl.ds(c, 1)] = gx[...][None, None]
    sixth = {}
    for d in y_order:
        sixth[d] = send(gx, gfull.at[y, c], s_gy.at[d], r_gy.at[d], y_peers[d])
        sent.append(sixth[d])
    seventh = [send(gx, gfull.at[y, c], s_gc.at[0], r_gc.at[0], partner)]
    for d in (1, 3, 2):
        sixth[d].wait_recv()
        src = lax.rem(y + NY - d, NY)
        seventh.append(send(gfull.at[src, c], gfull.at[src, c], s_gc.at[d], r_gc.at[d], partner))
    sent += seventh
    for copy in seventh:
        copy.wait_recv()

    tail = pl.ds(TERM_PAD - BLOCK, BLOCK)
    give_p = pltpu.make_async_remote_copy(
        src_ref=pbuf, dst_ref=pbuf, send_sem=s_swap.at[0], recv_sem=r_swap.at[0],
        device_id=partner, device_id_type=MESH,
    )
    give_y = pltpu.make_async_remote_copy(
        src_ref=ymat.at[tail, :], dst_ref=ymat.at[tail, :], send_sem=s_swap.at[1], recv_sem=r_swap.at[1],
        device_id=partner, device_id_type=MESH,
    )

    @pl.when(c == 0)
    def _():
        for k in range(NY):
            gram[K * k : K * k + K, :] = gfull[k].reshape(K, M)
        pbuf[...] = pod_rows(gram, aug_p, cinv)
        give_p.start()

    @pl.when(c == 1)
    def _():
        inverse_block(3 * BLOCK, amat, ymat, aug, linv)
        give_y.start()
        give_p.wait_recv()

    for d in z_order:
        fifth[d].wait_recv()
    p = pbuf[...]
    mine = mall.at[c, x]
    mall[pl.ds(c, 1), pl.ds(x, 1)] = nn(p, wfull[...].reshape(M, 128))[None, None]
    swaps = [send(mine, mine, s_mc.at[0], r_mc.at[0], partner)]
    moves = {}
    for d in (2, 1, 3):
        moves[d] = send(mine, mine, s_mx.at[d], r_mx.at[d], x_peers[d])
    loads[0].wait()
    for d in (1, 3, 2):
        moves[d].wait_recv()
        src = mall.at[c, lax.rem(x + NX - d, NX)]
        swaps.append(send(src, src, s_mc.at[d], r_mc.at[d], partner))
    for copy in swaps:
        copy.wait_recv()
    sent += swaps + list(moves.values())
    coeffs = jnp.concatenate([mall[k // NX, k % NX] for k in range(2 * NX)], axis=1)
    part = nt(coeffs, f_ref[...])
    half[...] = jnp.concatenate([part[:, 0:256], part[:, 256:]], axis=0).reshape(half.shape)
    rows = half.at[c]
    ry[pl.ds(y, 1)] = half[pl.ds(c, 1)]
    trade = {}
    for d in (2, 1, 3):
        trade[d] = send(rows, ry.at[y], s_y.at[d], r_y.at[d], y_peers[d])
    mc_out[...] = coeffs

    loads[1].wait()
    width = pod_out.shape[0]
    shift = lax.rem(NY - y, NY) * K
    picked = pltpu.roll(pbuf[pl.ds(pl.multiple_of(y * width, width), width), :] * scale, shift, 1)
    high, low = split(picked)
    upper = nn(jnp.concatenate([high, low], axis=0), parts_ref[0:M, :], None)
    pod_out[...] = (upper[0:width] + upper[width:]) + nn(high, parts_ref[M:, :], None)

    for d in (1, 3, 2):
        trade[d].wait_recv()
    rfull[pl.ds(c, 1)] = (((ry[0] + ry[1]) + ry[2]) + ry[3])[None]
    last = send(rfull.at[c], rfull.at[c], s_p.at[0], r_p.at[0], partner)

    @pl.when(c == 0)
    def _():
        give_y.wait_recv()

    last.wait_recv()
    sent += list(trade.values()) + [last]
    right = jnp.concatenate([rfull[0], rfull[1]], axis=1)
    surrogate = nn(nt(right, ymat[...]), ymat[...])
    fit_out[...] = nn(surrogate, f_ref[...])
    chaos_out[...] = chaos_scale * surrogate[:, 0 : chaos_out.shape[1]]

    @pl.when(c == 0)
    def _():
        give_p.wait_send()

    @pl.when(c == 1)
    def _():
        give_y.wait_send()

    for copy in sent:
        copy.wait_send()


def main(w, g, amat, ymat, f_local, parts, terms, scale, chaos_scale):
    f32 = jnp.float32
    dma = pltpu.SemaphoreType.DMA
    width = f_local.shape[1]
    cells = parts.shape[1]
    anywhere = pl.BlockSpec(memory_space=pl.ANY)
    square = pltpu.VMEM((TERM_PAD, TERM_PAD), f32)
    return pl.pallas_call(
        functools.partial(main_kernel, scale, chaos_scale),
        out_shape=(
            jax.ShapeDtypeStruct((K, width), f32),
            jax.ShapeDtypeStruct((K, width), f32),
            jax.ShapeDtypeStruct((K, terms), f32),
            jax.ShapeDtypeStruct((K // NY, cells), f32),
        ),
        in_specs=[VMEM, VMEM] + [anywhere] * 4,
        out_specs=(VMEM,) * 4,
        scratch_shapes=[
            pltpu.VMEM((NX, M, 128), f32),
            pltpu.VMEM((NX, 8, M), f32),
            pltpu.VMEM((NX, M, 128), f32),
            pltpu.VMEM((NX, 8, M), f32),
            pltpu.VMEM((NX, M, 128), f32),
            pltpu.VMEM((NX, 8, M), f32),
            pltpu.VMEM((NZ, M // NZ, 128), f32),
            pltpu.VMEM((NZ, M // NZ, 128), f32),
            pltpu.VMEM((NZ, 8, M), f32),
            pltpu.VMEM((NZ, M // NZ, 128), f32),
            pltpu.VMEM((NX, 8, M), f32),
            pltpu.VMEM((NY, 2, NX, 8, M), f32),
            square,
            square,
            *ELIMINATION,
            pltpu.VMEM((M, M), f32),
            pltpu.VMEM((K, 2 * K), f32),
            pltpu.VMEM((K, K), f32),
            pltpu.VMEM((K, M), f32),
            pltpu.VMEM((TERM_PAD, width), f32),
            pltpu.VMEM((2 * M, cells), jnp.bfloat16),
            pltpu.VMEM((2, NX, K, 128), f32),
            pltpu.VMEM((2, K, 256), f32),
            pltpu.VMEM((NY, K, 256), f32),
            pltpu.VMEM((2, K, 256), f32),
            dma((2, NX)), dma((2, NX)),
            dma((2, NX)), dma((2, NX)),
            dma((2, NZ)), dma((2, NZ)),
            dma((NZ,)), dma((NZ,)),
            dma((NX,)), dma((NX,)),
            dma((NY,)), dma((NY,)),
            dma((NY,)), dma((NY,)),
            dma((2,)), dma((2,)),
            dma((NX,)), dma((NX,)),
            dma((NX,)), dma((NX,)),
            dma((NY,)), dma((NY,)),
            dma((1,)), dma((1,)),
            dma((4,)),
        ],
        compiler_params=pltpu.CompilerParams(collective_id=0, has_side_effects=True),
        cost_estimate=cost(10**9, 10**7),
    )(w, g, amat, ymat, f_local, parts)


def local(snapshots, samples, sample_rates, sample_order, term_powers):
    own = snapshots.T
    up = [(i, (i + 1) % NY) for i in range(NY)]
    down = [(i, (i + NY - 1) % NY) for i in range(NY)]
    after = lax.ppermute(own, "col", down)
    before = lax.ppermute(own, "col", up)
    far = jnp.concatenate(
        [lax.ppermute(after[: K // 2], "col", down), lax.ppermute(before[K // 2 :], "col", up)], axis=0
    )

    total, terms = sample_rates.shape[0], term_powers.shape[0]
    pick_a, pick_b = selectors(term_powers.T)
    system, f_local = features_and_system(sample_rates.T, sample_order[None], pick_a, pick_b)
    amat, ymat = first_block(system)

    w_part, g_part, parts = partial_sums((own, after, far, before), samples)
    cell_count = snapshots.shape[0] * lax.axis_size("space")
    coeffs, fitted, chaos, pod_modes = main(
        w_part, g_part, amat, ymat, f_local, parts, terms, math.sqrt(cell_count), math.sqrt(total)
    )
    return (pod_modes.T, coeffs.T, fitted.T, chaos.T)


def solution(mesh):
    placed = (P("space", "col"), P("space", "col"), P(), P("col"), P())
    return jax.shard_map(
        local,
        mesh=mesh,
        in_specs=placed,
        out_specs=(P("space", "col"), P("col", None), P("col", None), P()),
        check_vma=False,
    )
```

```python
import functools
import itertools
import math

import jax
import jax.numpy as jnp
import numpy as np
from jax import lax
from jax.experimental import pallas as pl
from jax.experimental.pallas import tpu as pltpu
from jax.sharding import PartitionSpec as P

K = 64
M = 256
SWEEPS = 3
NX, NZ, NY = 4, 8, 4

top_degree = 4
ridge = 0.05

EXACT = lax.Precision.HIGHEST
TERM_PAD = 512
TABLE = 256
PART = 80
CHUNK = 1024
BLOCK = 128
MESH = pl.DeviceIdType.MESH
VMEM = pl.BlockSpec(memory_space=pltpu.VMEM)


def nn(a, b, precision=EXACT):
    return lax.dot_general(
        a, b, (((1,), (0,)), ((), ())), precision=precision, preferred_element_type=jnp.float32
    )


def nt(a, b, precision=EXACT):
    return lax.dot_general(
        a, b, (((1,), (1,)), ((), ())), precision=precision, preferred_element_type=jnp.float32
    )


def tn(a, b, precision=EXACT):
    return lax.dot_general(
        a, b, (((0,), (0,)), ((), ())), precision=precision, preferred_element_type=jnp.float32
    )


def cost(flops, bytes_accessed):
    return pl.CostEstimate(flops=flops, bytes_accessed=bytes_accessed, transcendentals=0)


def eye(n):
    rows = lax.broadcasted_iota(jnp.int32, (n, n), 0)
    return (rows == lax.broadcasted_iota(jnp.int32, (n, n), 1)).astype(jnp.float32)


def inverse_factor(aug, out, n):
    w = 2 * n
    groups = n // 8
    sub = lax.broadcasted_iota(jnp.int32, (8, w), 0)

    def body(b, carry):
        top = aug[0:8, :]
        r = [jnp.broadcast_to(top[k : k + 1, :], (8, w)) for k in range(8)]
        a = [[jnp.broadcast_to(r[i][:, j : j + 1], (8, w)) for j in range(i + 1)] for i in range(8)]
        low = [[None] * 8 for _ in range(8)]
        inv = [None] * 8
        for j in range(8):
            inv[j] = 1.0 / a[j][j]
            for i in range(j + 1, 8):
                low[i][j] = a[i][j] * inv[j]
            for i in range(j + 1, 8):
                for k in range(j + 1, i + 1):
                    a[i][k] = a[i][k] - low[i][j] * a[k][j]
                r[i] = r[i] - low[i][j] * r[j]
        q = [None] * 8
        for k in reversed(range(8)):
            v = r[k] * inv[k]
            for m in reversed(range(k + 1, 8)):
                v = v - low[m][k] * q[m]
            q[k] = v
        rows = r[0] * lax.rsqrt(a[0][0])
        for k in range(1, 8):
            rows = jnp.where(sub == k, r[k] * lax.rsqrt(a[k][k]), rows)
        out[pl.ds(pl.multiple_of(8 * b, 8), 8), :] = pltpu.roll(rows, 8 * b + n, 1)[:, :n]
        rest = aug[8:n, :].reshape(groups - 1, 8, w)
        upd = rest
        for k in range(8):
            upd = upd - jnp.broadcast_to(rest[:, :, k : k + 1], rest.shape) * q[k][None]
        aug[0 : n - 8, :] = pltpu.roll(upd.reshape(n - 8, w), w - 8, 1)
        return carry

    lax.fori_loop(0, groups, body, 0)


def pod_factor(m, aug, cinv):
    aug[...] = jnp.concatenate([m, eye(K)], axis=1)
    inverse_factor(aug, cinv, K)
    return cinv[...]


def pod_sweep(last, gram, zbuf, aug, cinv):
    z = zbuf[...]
    w = nn(z, gram[...])
    c = pod_factor(nt(z, w), aug, cinv)
    zbuf[...] = nn(c, z if last else w)


def combos():
    return [c for c in itertools.product(range(top_degree + 1), repeat=4) if sum(c) <= top_degree]


def table_codes():
    column = np.full((TABLE, 1), -1, np.int32)
    for m, c in enumerate(combos()):
        for part in range(3):
            column[PART * part + m] = sum(e * 5**i for i, e in enumerate(c))
    return jnp.asarray(column)


def selector(powers, codes):
    code = powers[0:1, :]
    for i in range(1, 4):
        code = code + powers[i : i + 1, :] * 5**i
    return jnp.where(codes == code, 1.0, 0.0).T.astype(jnp.bfloat16)


def fill_table(levels, first, parts, table):
    for m, c in enumerate(combos()):
        row = None
        for i, e in enumerate(c):
            if e:
                level = levels[e][first + i : first + i + 1, :]
                row = level if row is None else row * level
        table[m : m + 1, :] = jnp.ones_like(levels[1][0:1, :]) if row is None else row
    full = table[...]
    high = full.astype(jnp.bfloat16)
    left = full - high.astype(jnp.float32)
    mid = left.astype(jnp.bfloat16)
    parts[0:PART, :] = high
    parts[PART : 2 * PART, :] = mid
    parts[2 * PART : 3 * PART, :] = (left - mid.astype(jnp.float32)).astype(jnp.bfloat16)


def features(points, sa, sb, ta, tb, table):
    he = [jnp.ones_like(points), points]
    for d in range(1, top_degree):
        he.append(points * he[d] - d * he[d - 1])
    levels = [he[d] / math.sqrt(math.factorial(d)) for d in range(top_degree + 1)]
    fill_table(levels, 0, ta, table)
    fill_table(levels, 4, tb, table)
    return nn(sa[...], ta[...], None) * nn(sb[...], tb[...], None)


def picked_points(rates, order):
    total, width = rates.shape[1], order.shape[1]
    high = rates.astype(jnp.bfloat16).astype(jnp.float32)
    left = rates - high
    mid = left.astype(jnp.bfloat16).astype(jnp.float32)
    parts = jnp.concatenate([high, mid, left - mid, jnp.zeros_like(left)], axis=0).astype(jnp.bfloat16)
    piece = 512
    row = lax.broadcasted_iota(jnp.int32, (piece, width), 0)
    found = jnp.zeros((32, width), jnp.float32)
    for at in range(0, total, piece):
        hit = jnp.where(row == order - at, 1.0, 0.0).astype(jnp.bfloat16)
        found = found + nn(parts[:, at : at + piece], hit, None)
    return (found[0:8] + found[8:16]) + found[16:24]


def inverse_block(lo, amat, ymat, aug, linv):
    hi = lo + BLOCK
    aug[...] = jnp.concatenate([amat[lo:hi, lo:hi], eye(BLOCK)], axis=1)
    inverse_factor(aug, linv, BLOCK)
    li = linv[...]
    if lo:
        ymat[lo:hi, 0:lo] = nn(li, ymat[lo:hi, 0:lo])
    ymat[lo:hi, lo:hi] = li
    if hi < TERM_PAD:
        panel = nt(amat[hi:, lo:hi], li)
        amat[hi:, hi:] = amat[hi:, hi:] - nt(panel, panel)
        ymat[hi:, 0:hi] = ymat[hi:, 0:hi] - nn(panel, ymat[lo:hi, 0:hi])


ELIMINATION = [
    pltpu.VMEM((BLOCK, 2 * BLOCK), jnp.float32),
    pltpu.VMEM((BLOCK, BLOCK), jnp.float32),
]


def split(x):
    high = x.astype(jnp.bfloat16)
    return high, (x - high.astype(jnp.float32)).astype(jnp.bfloat16)


def place():
    s = lax.axis_index("space")
    return s // (NZ * 2), (s // 2) % NZ, s % 2, lax.axis_index("col")


def device(x, z, c, y):
    return {"space": (x * NZ + z) * 2 + c, "col": y}


def greet(peers):
    barrier = pltpu.get_barrier_semaphore()
    for peer in peers:
        pl.semaphore_signal(barrier, inc=1, device_id=peer, device_id_type=MESH)
    pl.semaphore_wait(barrier, len(peers))


def send(src, dst, send_sem, recv_sem, peer):
    copy = pltpu.make_async_remote_copy(
        src_ref=src,
        dst_ref=dst,
        send_sem=send_sem,
        recv_sem=recv_sem,
        device_id=peer,
        device_id_type=MESH,
    )
    copy.start()
    return copy


def lanes(k):
    return pl.ds(pl.multiple_of(k * 128, 128), 128)


def main_kernel(
    scale, chaos_scale,
    own_hbm, samples_hbm, rates_ref, order_ref, powers_ref, codes_ref,
    mc_out, fit_out, chaos_out, pod_out,
    shards, samples_ref, parts_ref, w_ref, g_ref,
    hh, hl, sa, sb, ta, tb, table,
    cw, cg, sxw, sxg, rxw, rxg, xw, zw, zg, wfull, gx, gfull,
    ymat, aug, linv, gram, aug_p, cinv, pbuf, f_ref,
    mall, half, ry, rfull,
    s_ag, r_ag,
    s_c, r_c, s_x, r_x, s_z, r_z, s_wz, r_wz, s_gx, r_gx, s_gy, r_gy, s_gc, r_gc,
    s_swap, r_swap, s_mx, r_mx, s_mc, r_mc, s_y, r_y, s_p, r_p, load,
):
    x, z, c, y = place()
    xs = [lax.rem(x + d, NX) for d in range(NX)]
    zs = [lax.rem(z + d, NZ) for d in range(NZ)]
    ys = [lax.rem(y + d, NY) for d in range(NY)]
    partner = device(x, z, 1 - c, y)
    x_peers = [device(xs[d], z, c, y) for d in range(NX)]
    z_peers = [device(x, zs[d], c, y) for d in range(NZ)]
    y_peers = [device(x, z, c, ys[d]) for d in range(NY)]
    x_order, z_order, y_order = (2, 1, 3, 0), (4, 3, 5, 2, 6, 1, 7), (2, 1, 3)
    loads = [
        pltpu.make_async_copy(own_hbm, shards.at[0], load.at[0]),
        pltpu.make_async_copy(samples_hbm, samples_ref, load.at[1]),
    ]
    greet([partner] + x_peers[1:] + z_peers[1:] + y_peers[1:])
    sent = []

    top, bottom = pl.ds(0, K // 2), pl.ds(K // 2, K // 2)
    near = {}
    for d, order in ((3, (top, bottom)), (1, (bottom, top))):
        slot = NY - d
        near[d] = [
            send(own_hbm.at[part, :], shards.at[slot, part, :], s_ag.at[d, i], r_ag.at[slot, i], y_peers[d])
            for i, part in enumerate(order)
        ]
        sent += near[d]
    for copy in loads:
        copy.start()

    hh[...] = jnp.zeros_like(hh)
    hl[...] = jnp.zeros_like(hl)
    ta[...] = jnp.zeros_like(ta)
    tb[...] = jnp.zeros_like(tb)
    table[...] = jnp.zeros_like(table)
    sa[...] = selector(powers_ref[0:4, :], codes_ref[...])
    sb[...] = selector(powers_ref[4:8, :], codes_ref[...])
    total = rates_ref.shape[1]

    def chunk(step, carry):
        v = rates_ref[:, pl.ds(pl.multiple_of(step * CHUNK, CHUNK), CHUNK)]
        high, low = split(features(v, sa, sb, ta, tb, table))
        hh[...] += nt(high, high, None)
        hl[...] += nt(high, low, None)
        return carry

    lax.fori_loop(0, total // CHUNK, chunk, 0)
    near[3][0].wait_recv()
    near[1][0].wait_recv()
    far = [
        send(shards.at[1, top, :], shards.at[2, top, :], s_ag.at[2, 0], r_ag.at[2, 0], y_peers[3]),
        send(shards.at[3, bottom, :], shards.at[2, bottom, :], s_ag.at[2, 1], r_ag.at[2, 1], y_peers[1]),
    ]
    sent += far
    f_ref[...] = features(picked_points(rates_ref[...], order_ref[...]), sa, sb, ta, tb, table)
    amat = hh
    amat[...] = hh[...] + hl[...] + hl[...].T + (ridge * total) * eye(TERM_PAD)
    ymat[...] = jnp.zeros_like(ymat)
    inverse_block(0, amat, ymat, aug, linv)
    inverse_block(BLOCK, amat, ymat, aug, linv)

    for copy in loads:
        copy.wait()
    near[3][1].wait_recv()
    near[1][1].wait_recv()
    slots = (0, 1, 3, 2)

    def take(first, count):
        for e in range(first, first + count):
            high, low = split(shards[slots[e]])
            parts_ref[2 * K * e : 2 * K * e + K, :] = high
            parts_ref[2 * K * e + K : 2 * K * (e + 1), :] = low

        def columns(n, carry):
            at = pl.ds(pl.multiple_of(n * 256, 256), 256)
            out = nn(parts_ref[2 * K * first : 2 * K * (first + count), :], samples_ref[:, at], None)
            for e in range(count):
                row = pl.multiple_of(ys[slots[first + e]] * K, K)
                w_ref[pl.ds(row, K), at] = out[2 * K * e : 2 * K * e + K] + out[2 * K * e + K : 2 * K * (e + 1)]
            return carry

        lax.fori_loop(0, samples_ref.shape[1] // 256, columns, 0)

    take(0, 3)
    for copy in far:
        copy.wait_recv()
    take(3, 1)
    grams = nt(parts_ref[0 : 2 * K, :], parts_ref[...], None)
    grams = grams[0:K] + grams[K:]
    blocks = [grams[:, 2 * K * e : 2 * K * e + K] + grams[:, 2 * K * e + K : 2 * K * (e + 1)] for e in (0, 1, 3, 2)]
    g_ref[...] = pltpu.roll(jnp.concatenate(blocks, axis=1), y * K, 1)

    first = {}
    for d in x_order:
        other = (1 - c) * NX + xs[d]
        rows = pl.ds(pl.multiple_of(other * 8, 8), 8)
        first[d] = (
            send(g_ref.at[rows, :], cg.at[d], s_c.at[0, d], r_c.at[0, d], partner),
            send(w_ref.at[:, lanes(other)], cw.at[d], s_c.at[1, d], r_c.at[1, d], partner),
        )
        sent += first[d]
    second = {}
    for d in x_order:
        mine = c * NX + xs[d]
        for copy in first[d]:
            copy.wait_recv()
        gsum = g_ref[pl.ds(pl.multiple_of(mine * 8, 8), 8), :] + cg[d]
        wsum = w_ref[:, lanes(mine)] + cw[d]
        if d:
            sxg[d] = gsum
            sxw[d] = wsum
            second[d] = (
                send(sxg.at[d], rxg.at[x], s_x.at[0, d], r_x.at[0, d], x_peers[d]),
                send(sxw.at[d], rxw.at[x], s_x.at[1, d], r_x.at[1, d], x_peers[d]),
            )
            sent += second[d]
        else:
            rxg[pl.ds(x, 1)] = gsum[None]
            rxw[pl.ds(x, 1)] = wsum[None]

    for d in (1, 3, 2):
        second[d][0].wait_recv()
    sxg[0] = ((rxg[0] + rxg[1]) + rxg[2]) + rxg[3]
    zg[pl.ds(z, 1)] = sxg[0][None]
    third = {}
    for d in z_order:
        third[d] = [send(sxg.at[0], zg.at[z], s_z.at[0, d], r_z.at[0, d], z_peers[d])]
    for d in z_order:
        third[d][0].wait_recv()
    total = zg[0]
    for k in range(1, NZ):
        total = total + zg[k]
    gx[pl.ds(x, 1)] = total[None]
    fourth = {}
    for d in (2, 1, 3):
        fourth[d] = send(gx.at[x], gx.at[x], s_gx.at[d], r_gx.at[d], x_peers[d])
        sent.append(fourth[d])

    for d in (1, 3, 2):
        second[d][1].wait_recv()
    xw[...] = (((rxw[0] + rxw[1]) + rxw[2]) + rxw[3]).reshape(xw.shape)
    for d in z_order:
        third[d].append(send(xw.at[zs[d]], zw.at[z], s_z.at[1, d], r_z.at[1, d], z_peers[d]))
        sent += third[d]
    zw[pl.ds(z, 1)] = xw[pl.ds(z, 1)]

    for d in (1, 3, 2):
        fourth[d].wait_recv()
    gfull[pl.ds(y, 1), pl.ds(c, 1)] = gx[...][None, None]
    sixth = {}
    for d in y_order:
        sixth[d] = send(gx, gfull.at[y, c], s_gy.at[d], r_gy.at[d], y_peers[d])
        sent.append(sixth[d])
    seventh = [send(gx, gfull.at[y, c], s_gc.at[0], r_gc.at[0], partner)]
    for d in (1, 3, 2):
        sixth[d].wait_recv()
        src = lax.rem(y + NY - d, NY)
        seventh.append(send(gfull.at[src, c], gfull.at[src, c], s_gc.at[d], r_gc.at[d], partner))
    sent += seventh
    for copy in seventh:
        copy.wait_recv()

    tail = pl.ds(TERM_PAD - 2 * BLOCK, 2 * BLOCK)
    give_p = pltpu.make_async_remote_copy(
        src_ref=pbuf, dst_ref=pbuf, send_sem=s_swap.at[0], recv_sem=r_swap.at[0],
        device_id=partner, device_id_type=MESH,
    )
    give_y = pltpu.make_async_remote_copy(
        src_ref=ymat.at[tail, :], dst_ref=ymat.at[tail, :], send_sem=s_swap.at[1], recv_sem=r_swap.at[1],
        device_id=partner, device_id_type=MESH,
    )

    @pl.when(c == 0)
    def _():
        for k in range(NY):
            gram[K * k : K * k + K, :] = gfull[k].reshape(K, M)
        pbuf[...] = nn(pod_factor(gram[0:K, 0:K], aug_p, cinv), gram[0:K, :])
        pod_sweep(False, gram, pbuf, aug_p, cinv)

    @pl.when(c == 1)
    def _():
        inverse_block(2 * BLOCK, amat, ymat, aug, linv)

    for d in z_order:
        third[d][1].wait_recv()
    total = zw[0]
    for k in range(1, NZ):
        total = total + zw[k]
    wfull[pl.ds(z, 1)] = total[None]
    fifth = {}
    for d in z_order:
        fifth[d] = send(wfull.at[z], wfull.at[z], s_wz.at[d], r_wz.at[d], z_peers[d])
        sent.append(fifth[d])

    @pl.when(c == 0)
    def _():
        pod_sweep(False, gram, pbuf, aug_p, cinv)
        pod_sweep(True, gram, pbuf, aug_p, cinv)
        give_p.start()

    @pl.when(c == 1)
    def _():
        inverse_block(3 * BLOCK, amat, ymat, aug, linv)
        give_y.start()
        give_p.wait_recv()

    for d in z_order:
        fifth[d].wait_recv()
    p = pbuf[...]
    mine = mall.at[c, x]
    mall[pl.ds(c, 1), pl.ds(x, 1)] = nn(p, wfull[...].reshape(M, 128))[None, None]
    swaps = [send(mine, mine, s_mc.at[0], r_mc.at[0], partner)]
    moves = {}
    for d in (2, 1, 3):
        moves[d] = send(mine, mine, s_mx.at[d], r_mx.at[d], x_peers[d])
    for d in (1, 3, 2):
        moves[d].wait_recv()
        src = mall.at[c, lax.rem(x + NX - d, NX)]
        swaps.append(send(src, src, s_mc.at[d], r_mc.at[d], partner))
    for copy in swaps:
        copy.wait_recv()
    sent += swaps + list(moves.values())
    coeffs = jnp.concatenate([mall[k // NX, k % NX] for k in range(2 * NX)], axis=1)
    part = nt(coeffs, f_ref[...])
    half[...] = jnp.concatenate([part[:, 0:256], part[:, 256:]], axis=0).reshape(half.shape)
    rows = half.at[c]
    ry[pl.ds(y, 1)] = half[pl.ds(c, 1)]
    trade = {}
    for d in (2, 1, 3):
        trade[d] = send(rows, ry.at[y], s_y.at[d], r_y.at[d], y_peers[d])
    mc_out[...] = coeffs

    width = pod_out.shape[0]
    shift = lax.rem(NY - y, NY) * K
    picked = pltpu.roll(pbuf[pl.ds(pl.multiple_of(y * width, width), width), :] * scale, shift, 1)
    cuts = [picked[:, K * d : K * d + K] for d in slots]
    picked = jnp.concatenate([cuts[e // 2] for e in range(2 * NY)], axis=1)
    outer = nn(jnp.concatenate(split(picked), axis=0), parts_ref[...], None)
    pod_out[...] = outer[0:width] + outer[width:]

    for d in (1, 3, 2):
        trade[d].wait_recv()
    rfull[pl.ds(c, 1)] = (((ry[0] + ry[1]) + ry[2]) + ry[3])[None]
    last = send(rfull.at[c], rfull.at[c], s_p.at[0], r_p.at[0], partner)

    @pl.when(c == 0)
    def _():
        give_y.wait_recv()

    last.wait_recv()
    sent += list(trade.values()) + [last]
    right = jnp.concatenate([rfull[0], rfull[1]], axis=1)
    surrogate = nn(nt(right, ymat[...]), ymat[...])
    fit_out[...] = nn(surrogate, f_ref[...])
    chaos_out[...] = chaos_scale * surrogate[:, 0 : chaos_out.shape[1]]

    @pl.when(c == 0)
    def _():
        give_p.wait_send()

    @pl.when(c == 1)
    def _():
        give_y.wait_send()

    for copy in sent:
        copy.wait_send()


def main(own, samples, rates_t, order, powers, terms, scale, chaos_scale):
    f32, bf16 = jnp.float32, jnp.bfloat16
    dma = pltpu.SemaphoreType.DMA
    cells, width = samples.shape
    anywhere = pl.BlockSpec(memory_space=pl.ANY)
    square = pltpu.VMEM((TERM_PAD, TERM_PAD), f32)
    return pl.pallas_call(
        functools.partial(main_kernel, scale, chaos_scale),
        out_shape=(
            jax.ShapeDtypeStruct((K, width), f32),
            jax.ShapeDtypeStruct((K, width), f32),
            jax.ShapeDtypeStruct((K, terms), f32),
            jax.ShapeDtypeStruct((K // NY, cells), f32),
        ),
        in_specs=[anywhere] * 2 + [VMEM] * 4,
        out_specs=(VMEM,) * 4,
        scratch_shapes=[
            pltpu.VMEM((NY, K, cells), f32),
            pltpu.VMEM((cells, width), bf16),
            pltpu.VMEM((2 * M, cells), bf16),
            pltpu.VMEM((M, width), f32),
            pltpu.VMEM((K, M), f32),
            square,
            square,
            pltpu.VMEM((TERM_PAD, TABLE), bf16),
            pltpu.VMEM((TERM_PAD, TABLE), bf16),
            pltpu.VMEM((TABLE, CHUNK), bf16),
            pltpu.VMEM((TABLE, CHUNK), bf16),
            pltpu.VMEM((PART, CHUNK), f32),
            pltpu.VMEM((NX, M, 128), f32),
            pltpu.VMEM((NX, 8, M), f32),
            pltpu.VMEM((NX, M, 128), f32),
            pltpu.VMEM((NX, 8, M), f32),
            pltpu.VMEM((NX, M, 128), f32),
            pltpu.VMEM((NX, 8, M), f32),
            pltpu.VMEM((NZ, M // NZ, 128), f32),
            pltpu.VMEM((NZ, M // NZ, 128), f32),
            pltpu.VMEM((NZ, 8, M), f32),
            pltpu.VMEM((NZ, M // NZ, 128), f32),
            pltpu.VMEM((NX, 8, M), f32),
            pltpu.VMEM((NY, 2, NX, 8, M), f32),
            square,
            *ELIMINATION,
            pltpu.VMEM((M, M), f32),
            pltpu.VMEM((K, 2 * K), f32),
            pltpu.VMEM((K, K), f32),
            pltpu.VMEM((K, M), f32),
            pltpu.VMEM((TERM_PAD, width), f32),
            pltpu.VMEM((2, NX, K, 128), f32),
            pltpu.VMEM((2, K, 256), f32),
            pltpu.VMEM((NY, K, 256), f32),
            pltpu.VMEM((2, K, 256), f32),
            dma((NY, 2)), dma((NY, 2)),
            dma((2, NX)), dma((2, NX)),
            dma((2, NX)), dma((2, NX)),
            dma((2, NZ)), dma((2, NZ)),
            dma((NZ,)), dma((NZ,)),
            dma((NX,)), dma((NX,)),
            dma((NY,)), dma((NY,)),
            dma((NY,)), dma((NY,)),
            dma((2,)), dma((2,)),
            dma((NX,)), dma((NX,)),
            dma((NX,)), dma((NX,)),
            dma((NY,)), dma((NY,)),
            dma((1,)), dma((1,)),
            dma((2,)),
        ],
        compiler_params=pltpu.CompilerParams(
            collective_id=0, has_side_effects=True, vmem_limit_bytes=60 * 2**20
        ),
        cost_estimate=cost(10**11, 2 * 10**7),
    )(own, samples, rates_t, order, powers, table_codes())


def hand_over_kernel(*refs):
    count = len(refs) // 2
    for src, dst in zip(refs[:count], refs[count:]):
        dst[...] = src[...]


def hand_over(arrays):
    return pl.pallas_call(
        hand_over_kernel,
        out_shape=tuple(jax.ShapeDtypeStruct(a.shape, a.dtype) for a in arrays),
        in_specs=[VMEM] * len(arrays),
        out_specs=(VMEM,) * len(arrays),
    )(*arrays)


def local(snapshots, samples, sample_rates, sample_order, term_powers):
    total, terms = sample_rates.shape[0], term_powers.shape[0]
    cell_count = snapshots.shape[0] * lax.axis_size("space")
    powers = jnp.pad(term_powers.T, ((0, 0), (0, TERM_PAD - terms)), constant_values=-1)
    outs = main(
        snapshots.T, samples, sample_rates.T, sample_order[None], powers,
        terms, math.sqrt(cell_count), math.sqrt(total),
    )
    coeffs, fitted, chaos, pod_modes = hand_over(outs)
    return (pod_modes.T, coeffs.T, fitted.T, chaos.T)


def solution(mesh):
    placed = (P("space", "col"), P("space", "col"), P(), P("col"), P())
    return jax.shard_map(
        local,
        mesh=mesh,
        in_specs=placed,
        out_specs=(P("space", "col"), P("col", None), P("col", None), P()),
        check_vma=False,
    )
```

```python
import functools
import itertools
import math

import jax
import jax.numpy as jnp
import numpy as np
from jax import lax
from jax.experimental import pallas as pl
from jax.experimental.pallas import tpu as pltpu
from jax.sharding import PartitionSpec as P

K = 64
M = 256
SWEEPS = 3
NX, NZ, NY = 4, 8, 4

top_degree = 4
ridge = 0.05

EXACT = lax.Precision.HIGHEST
TERM_PAD = 512
TABLE = 256
PART = 80
CHUNK = 1024
PIECES = 4
BLOCK = 128
MESH = pl.DeviceIdType.MESH
VMEM = pl.BlockSpec(memory_space=pltpu.VMEM)


def nn(a, b, precision=EXACT):
    return lax.dot_general(
        a, b, (((1,), (0,)), ((), ())), precision=precision, preferred_element_type=jnp.float32
    )


def nt(a, b, precision=EXACT):
    return lax.dot_general(
        a, b, (((1,), (1,)), ((), ())), precision=precision, preferred_element_type=jnp.float32
    )


def tn(a, b, precision=EXACT):
    return lax.dot_general(
        a, b, (((0,), (0,)), ((), ())), precision=precision, preferred_element_type=jnp.float32
    )


def cost(flops, bytes_accessed):
    return pl.CostEstimate(flops=flops, bytes_accessed=bytes_accessed, transcendentals=0)


def eye(n):
    rows = lax.broadcasted_iota(jnp.int32, (n, n), 0)
    return (rows == lax.broadcasted_iota(jnp.int32, (n, n), 1)).astype(jnp.float32)


def pivot_block(top, at, w):
    r = [jnp.broadcast_to(top[k : k + 1, :], (8, w)) for k in range(8)]
    a = [
        [jnp.broadcast_to(r[i][:, at + j : at + j + 1], (8, w)) for j in range(i + 1)] for i in range(8)
    ]
    s = [[None] * 8 for _ in range(8)]
    inv = [None] * 8
    for j in range(8):
        inv[j] = lax.rsqrt(a[j][j])
        r[j] = r[j] * inv[j]
        for i in range(j + 1, 8):
            s[i][j] = a[i][j] * inv[j]
        for i in range(j + 1, 8):
            for k in range(j + 1, i + 1):
                a[i][k] = a[i][k] - s[i][j] * s[k][j]
            r[i] = r[i] - s[i][j] * r[j]
    q = [None] * 8
    for k in reversed(range(8)):
        v = r[k]
        for m in reversed(range(k + 1, 8)):
            v = v - s[m][k] * q[m]
        q[k] = v * inv[k]
    return r, q


def merge_rows(r, w):
    sub = lax.broadcasted_iota(jnp.int32, (8, w), 0)
    rows = r[0]
    for k in range(1, 8):
        rows = jnp.where(sub == k, r[k], rows)
    return rows


def inverse_factor(aug, out, n):
    w = 2 * n
    groups = n // 8

    def body(b, carry):
        r, q = pivot_block(aug[0:8, :], 0, w)
        out[pl.ds(pl.multiple_of(8 * b, 8), 8), :] = pltpu.roll(merge_rows(r, w), 8 * b + n, 1)[:, :n]
        rest = aug[8:n, :].reshape(groups - 1, 8, w)
        upd = rest
        for k in range(8):
            upd = upd - jnp.broadcast_to(rest[:, :, k : k + 1], rest.shape) * q[k][None]
        aug[0 : n - 8, :] = pltpu.roll(upd.reshape(n - 8, w), w - 8, 1)
        return carry

    lax.fori_loop(0, groups, body, 0)


def pod_factor(m, aug, cinv):
    aug[...] = jnp.concatenate([m, eye(K)], axis=1)
    inverse_factor(aug, cinv, K)
    return cinv[...]


def pod_sweep(last, gram, zbuf, aug, cinv):
    z = zbuf[...]
    w = nn(z, gram[...])
    c = pod_factor(nt(z, w), aug, cinv)
    zbuf[...] = nn(c, z if last else w)


def combos():
    return [c for c in itertools.product(range(top_degree + 1), repeat=4) if sum(c) <= top_degree]


def table_codes():
    column = np.full((TABLE, 1), -1, np.int32)
    for m, c in enumerate(combos()):
        for part in range(3):
            column[PART * part + m] = sum(e * 5**i for i, e in enumerate(c))
    return jnp.asarray(column)


def selector(powers, codes):
    code = powers[0:1, :]
    for i in range(1, 4):
        code = code + powers[i : i + 1, :] * 5**i
    return jnp.where(codes == code, 1.0, 0.0).T.astype(jnp.bfloat16)


def fill_table(levels, first, parts, table):
    for m, c in enumerate(combos()):
        row = None
        for i, e in enumerate(c):
            if e:
                level = levels[e][first + i : first + i + 1, :]
                row = level if row is None else row * level
        table[m : m + 1, :] = jnp.ones_like(levels[1][0:1, :]) if row is None else row
    full = table[...]
    high = full.astype(jnp.bfloat16)
    left = full - high.astype(jnp.float32)
    mid = left.astype(jnp.bfloat16)
    parts[0:PART, :] = high
    parts[PART : 2 * PART, :] = mid
    parts[2 * PART : 3 * PART, :] = (left - mid.astype(jnp.float32)).astype(jnp.bfloat16)


def features(points, sa, sb, ta, tb, table):
    he = [jnp.ones_like(points), points]
    for d in range(1, top_degree):
        he.append(points * he[d] - d * he[d - 1])
    levels = [he[d] / math.sqrt(math.factorial(d)) for d in range(top_degree + 1)]
    fill_table(levels, 0, ta, table)
    fill_table(levels, 4, tb, table)
    return nn(sa[...], ta[...], None) * nn(sb[...], tb[...], None)


def picked_points(rates, order):
    total, width = rates.shape[1], order.shape[1]
    high = rates.astype(jnp.bfloat16).astype(jnp.float32)
    left = rates - high
    mid = left.astype(jnp.bfloat16).astype(jnp.float32)
    parts = jnp.concatenate([high, mid, left - mid, jnp.zeros_like(left)], axis=0).astype(jnp.bfloat16)
    piece = 512
    row = lax.broadcasted_iota(jnp.int32, (piece, width), 0)
    found = jnp.zeros((32, width), jnp.float32)
    for at in range(0, total, piece):
        hit = jnp.where(row == order - at, 1.0, 0.0).astype(jnp.bfloat16)
        found = found + nn(parts[:, at : at + piece], hit, None)
    return (found[0:8] + found[8:16]) + found[16:24]


def inverse_block(lo, amat, ymat, aug, linv):
    hi = lo + BLOCK
    aug[...] = jnp.concatenate([amat[lo:hi, lo:hi], eye(BLOCK)], axis=1)
    inverse_factor(aug, linv, BLOCK)
    li = linv[...]
    if lo:
        ymat[lo:hi, 0:lo] = nn(li, ymat[lo:hi, 0:lo])
    ymat[lo:hi, lo:hi] = li
    if hi < TERM_PAD:
        panel = nt(amat[hi:, lo:hi], li)
        amat[hi:, hi:] = amat[hi:, hi:] - nt(panel, panel)
        ymat[hi:, 0:hi] = ymat[hi:, 0:hi] - nn(panel, ymat[lo:hi, 0:hi])


ELIMINATION = [
    pltpu.VMEM((BLOCK, 2 * BLOCK), jnp.float32),
    pltpu.VMEM((BLOCK, BLOCK), jnp.float32),
]


def split(x):
    high = x.astype(jnp.bfloat16)
    return high, (x - high.astype(jnp.float32)).astype(jnp.bfloat16)


def partial_products(i, piece, slots, shards, samples_ref, parts_ref, acc, gacc):
    both = jnp.concatenate([half for e in range(NY) for half in split(shards[slots[e], :, piece])], axis=0)
    parts_ref[:, piece] = both
    out = nn(both, samples_ref[piece, :], None)
    gram = nt(both[0 : 2 * K], both, None)
    if i:
        acc[...] += out
        gacc[...] += gram
    else:
        acc[...] = out
        gacc[...] = gram


def place():
    s = lax.axis_index("space")
    return s // (NZ * 2), (s // 2) % NZ, s % 2, lax.axis_index("col")


def device(x, z, c, y):
    return {"space": (x * NZ + z) * 2 + c, "col": y}


def greet(peers):
    barrier = pltpu.get_barrier_semaphore()
    for peer in peers:
        pl.semaphore_signal(barrier, inc=1, device_id=peer, device_id_type=MESH)
    pl.semaphore_wait(barrier, len(peers))


def send(src, dst, send_sem, recv_sem, peer):
    copy = pltpu.make_async_remote_copy(
        src_ref=src,
        dst_ref=dst,
        send_sem=send_sem,
        recv_sem=recv_sem,
        device_id=peer,
        device_id_type=MESH,
    )
    copy.start()
    return copy


def lanes(k):
    return pl.ds(pl.multiple_of(k * 128, 128), 128)


def main_kernel(
    scale, chaos_scale,
    own_hbm, samples_hbm, rates_ref, order_ref, powers_ref, codes_ref,
    mc_out, fit_out, chaos_out, pod_out,
    shards, samples_ref, parts_ref, acc, gacc, w_ref, g_ref,
    hh, hl, powers, sa, sb, ta, tb, table,
    cw, cg, sxw, sxg, rxw, rxg, xw, zw, zg, wfull, gx, gfull,
    ymat, aug, linv, gram, aug_p, cinv, pbuf, f_ref,
    mall, half, ry, rfull,
    s_ag, r_ag,
    s_c, r_c, s_x, r_x, s_z, r_z, s_wz, r_wz, s_gx, r_gx, s_gy, r_gy, s_gc, r_gc,
    s_swap, r_swap, s_mx, r_mx, s_mc, r_mc, s_y, r_y, s_p, r_p, load,
):
    x, z, c, y = place()
    xs = [lax.rem(x + d, NX) for d in range(NX)]
    zs = [lax.rem(z + d, NZ) for d in range(NZ)]
    ys = [lax.rem(y + d, NY) for d in range(NY)]
    partner = device(x, z, 1 - c, y)
    x_peers = [device(xs[d], z, c, y) for d in range(NX)]
    z_peers = [device(x, zs[d], c, y) for d in range(NZ)]
    y_peers = [device(x, z, c, ys[d]) for d in range(NY)]
    x_order, z_order, y_order = (2, 1, 3, 0), (4, 3, 5, 2, 6, 1, 7), (2, 1, 3)
    loads = [
        pltpu.make_async_copy(own_hbm, shards.at[0], load.at[0]),
        pltpu.make_async_copy(samples_hbm, samples_ref, load.at[1]),
    ]
    greet([partner] + x_peers[1:] + z_peers[1:] + y_peers[1:])
    sent = []

    top, bottom = pl.ds(0, K // 2), pl.ds(K // 2, K // 2)
    cells = samples_ref.shape[0]
    pieces = [pl.ds(at, cells // PIECES) for at in range(0, cells, cells // PIECES)]
    near = {}
    for i, piece in enumerate(pieces):
        for d in (3, 1):
            slot = NY - d
            near[d, i] = send(
                own_hbm.at[:, piece], shards.at[slot, :, piece], s_ag.at[d, i], r_ag.at[slot, i], y_peers[d]
            )
            sent.append(near[d, i])
    far = {}

    def relay(i):
        for h, (d, src, part) in enumerate(((3, 1, top), (1, 3, bottom))):
            near[d, i].wait_recv()
            far[h, i] = send(
                shards.at[src, part, pieces[i]], shards.at[2, part, pieces[i]],
                s_ag.at[2 * h, PIECES + i], r_ag.at[2 * h, PIECES + i], y_peers[d],
            )
            sent.append(far[h, i])

    for copy in loads:
        copy.start()

    hh[...] = jnp.zeros_like(hh)
    hl[...] = jnp.zeros_like(hl)
    ta[...] = jnp.zeros_like(ta)
    tb[...] = jnp.zeros_like(tb)
    table[...] = jnp.zeros_like(table)
    powers[...] = jnp.full_like(powers, -1)
    powers[:, 0 : powers_ref.shape[1]] = powers_ref[...]
    sa[...] = selector(powers[0:4, :], codes_ref[...])
    sb[...] = selector(powers[4:8, :], codes_ref[...])
    total = rates_ref.shape[1]

    def chunk(step, carry):
        v = rates_ref[:, pl.ds(pl.multiple_of(step * CHUNK, CHUNK), CHUNK)]
        high, low = split(features(v, sa, sb, ta, tb, table))
        hh[...] += nt(high, high, None)
        hl[...] += nt(high, low, None)
        return carry

    lax.fori_loop(0, total // CHUNK, chunk, 0)
    relay(0)
    relay(1)
    f_ref[...] = features(picked_points(rates_ref[...], order_ref[...]), sa, sb, ta, tb, table)
    amat = hh
    amat[...] = hh[...] + hl[...] + hl[...].T + (ridge * total) * eye(TERM_PAD)
    ymat[...] = jnp.zeros_like(ymat)
    inverse_block(0, amat, ymat, aug, linv)
    relay(2)
    inverse_block(BLOCK, amat, ymat, aug, linv)
    relay(3)

    for copy in loads:
        copy.wait()
    slots = (0, 1, 3, 2)
    for i, piece in enumerate(pieces):
        far[0, i].wait_recv()
        far[1, i].wait_recv()
        partial_products(i, piece, slots, shards, samples_ref, parts_ref, acc, gacc)
    for e in range(NY):
        row = pl.multiple_of(ys[slots[e]] * K, K)
        lo = 2 * K * e
        w_ref[pl.ds(row, K), :] = acc[lo : lo + K, :] + acc[lo + K : lo + 2 * K, :]
    grams = gacc[0:K, :] + gacc[K:, :]
    blocks = [grams[:, 2 * K * e : 2 * K * e + K] + grams[:, 2 * K * e + K : 2 * K * (e + 1)] for e in (0, 1, 3, 2)]
    g_ref[...] = pltpu.roll(jnp.concatenate(blocks, axis=1), y * K, 1)

    first = {}
    for d in x_order:
        other = (1 - c) * NX + xs[d]
        rows = pl.ds(pl.multiple_of(other * 8, 8), 8)
        first[d] = (
            send(g_ref.at[rows, :], cg.at[d], s_c.at[0, d], r_c.at[0, d], partner),
            send(w_ref.at[:, lanes(other)], cw.at[d], s_c.at[1, d], r_c.at[1, d], partner),
        )
        sent += first[d]
    second = {}
    for d in x_order:
        mine = c * NX + xs[d]
        for copy in first[d]:
            copy.wait_recv()
        gsum = g_ref[pl.ds(pl.multiple_of(mine * 8, 8), 8), :] + cg[d]
        wsum = w_ref[:, lanes(mine)] + cw[d]
        if d:
            sxg[d] = gsum
            sxw[d] = wsum
            second[d] = (
                send(sxg.at[d], rxg.at[x], s_x.at[0, d], r_x.at[0, d], x_peers[d]),
                send(sxw.at[d], rxw.at[x], s_x.at[1, d], r_x.at[1, d], x_peers[d]),
            )
            sent += second[d]
        else:
            rxg[pl.ds(x, 1)] = gsum[None]
            rxw[pl.ds(x, 1)] = wsum[None]

    for d in (1, 3, 2):
        second[d][0].wait_recv()
    sxg[0] = ((rxg[0] + rxg[1]) + rxg[2]) + rxg[3]
    zg[pl.ds(z, 1)] = sxg[0][None]
    third = {}
    for d in z_order:
        third[d] = [send(sxg.at[0], zg.at[z], s_z.at[0, d], r_z.at[0, d], z_peers[d])]
    for d in z_order:
        third[d][0].wait_recv()
    total = zg[0]
    for k in range(1, NZ):
        total = total + zg[k]
    gx[pl.ds(x, 1)] = total[None]
    fourth = {}
    for d in (2, 1, 3):
        fourth[d] = send(gx.at[x], gx.at[x], s_gx.at[d], r_gx.at[d], x_peers[d])
        sent.append(fourth[d])

    for d in (1, 3, 2):
        second[d][1].wait_recv()
    xw[...] = (((rxw[0] + rxw[1]) + rxw[2]) + rxw[3]).reshape(xw.shape)
    for d in z_order:
        third[d].append(send(xw.at[zs[d]], zw.at[z], s_z.at[1, d], r_z.at[1, d], z_peers[d]))
        sent += third[d]
    zw[pl.ds(z, 1)] = xw[pl.ds(z, 1)]

    for d in (1, 3, 2):
        fourth[d].wait_recv()
    gfull[pl.ds(y, 1), pl.ds(c, 1)] = gx[...][None, None]
    sixth = {}
    for d in y_order:
        sixth[d] = send(gx, gfull.at[y, c], s_gy.at[d], r_gy.at[d], y_peers[d])
        sent.append(sixth[d])
    seventh = [send(gx, gfull.at[y, c], s_gc.at[0], r_gc.at[0], partner)]
    for d in (1, 3, 2):
        sixth[d].wait_recv()
        src = lax.rem(y + NY - d, NY)
        seventh.append(send(gfull.at[src, c], gfull.at[src, c], s_gc.at[d], r_gc.at[d], partner))
    sent += seventh
    for copy in seventh:
        copy.wait_recv()

    tail = pl.ds(TERM_PAD - 2 * BLOCK, 2 * BLOCK)
    give_p = pltpu.make_async_remote_copy(
        src_ref=pbuf, dst_ref=pbuf, send_sem=s_swap.at[0], recv_sem=r_swap.at[0],
        device_id=partner, device_id_type=MESH,
    )
    give_y = pltpu.make_async_remote_copy(
        src_ref=ymat.at[tail, :], dst_ref=ymat.at[tail, :], send_sem=s_swap.at[1], recv_sem=r_swap.at[1],
        device_id=partner, device_id_type=MESH,
    )

    @pl.when(c == 0)
    def _():
        for k in range(NY):
            gram[K * k : K * k + K, :] = gfull[k].reshape(K, M)
        pbuf[...] = nn(pod_factor(gram[0:K, 0:K], aug_p, cinv), gram[0:K, :])
        pod_sweep(False, gram, pbuf, aug_p, cinv)

    @pl.when(c == 1)
    def _():
        inverse_block(2 * BLOCK, amat, ymat, aug, linv)

    for d in z_order:
        third[d][1].wait_recv()
    total = zw[0]
    for k in range(1, NZ):
        total = total + zw[k]
    wfull[pl.ds(z, 1)] = total[None]
    fifth = {}
    for d in z_order:
        fifth[d] = send(wfull.at[z], wfull.at[z], s_wz.at[d], r_wz.at[d], z_peers[d])
        sent.append(fifth[d])

    @pl.when(c == 0)
    def _():
        pod_sweep(False, gram, pbuf, aug_p, cinv)
        pod_sweep(True, gram, pbuf, aug_p, cinv)
        give_p.start()

    @pl.when(c == 1)
    def _():
        inverse_block(3 * BLOCK, amat, ymat, aug, linv)
        give_y.start()
        give_p.wait_recv()

    for d in z_order:
        fifth[d].wait_recv()
    p = pbuf[...]
    mine = mall.at[c, x]
    mall[pl.ds(c, 1), pl.ds(x, 1)] = nn(p, wfull[...].reshape(M, 128))[None, None]
    swaps = [send(mine, mine, s_mc.at[0], r_mc.at[0], partner)]
    moves = {}
    for d in (2, 1, 3):
        moves[d] = send(mine, mine, s_mx.at[d], r_mx.at[d], x_peers[d])
    for d in (1, 3, 2):
        moves[d].wait_recv()
        src = mall.at[c, lax.rem(x + NX - d, NX)]
        swaps.append(send(src, src, s_mc.at[d], r_mc.at[d], partner))
    for copy in swaps:
        copy.wait_recv()
    sent += swaps + list(moves.values())
    coeffs = jnp.concatenate([mall[k // NX, k % NX] for k in range(2 * NX)], axis=1)
    part = nt(coeffs, f_ref[...])
    half[...] = jnp.concatenate([part[:, 0:256], part[:, 256:]], axis=0).reshape(half.shape)
    rows = half.at[c]
    ry[pl.ds(y, 1)] = half[pl.ds(c, 1)]
    trade = {}
    for d in (2, 1, 3):
        trade[d] = send(rows, ry.at[y], s_y.at[d], r_y.at[d], y_peers[d])
    mc_out[...] = coeffs

    width = pod_out.shape[0]
    shift = lax.rem(NY - y, NY) * K
    picked = pltpu.roll(pbuf[pl.ds(pl.multiple_of(y * width, width), width), :] * scale, shift, 1)
    cuts = [picked[:, K * d : K * d + K] for d in slots]
    picked = jnp.concatenate([cuts[e // 2] for e in range(2 * NY)], axis=1)
    outer = nn(jnp.concatenate(split(picked), axis=0), parts_ref[...], None)
    pod_out[...] = outer[0:width] + outer[width:]

    for d in (1, 3, 2):
        trade[d].wait_recv()
    rfull[pl.ds(c, 1)] = (((ry[0] + ry[1]) + ry[2]) + ry[3])[None]
    last = send(rfull.at[c], rfull.at[c], s_p.at[0], r_p.at[0], partner)

    @pl.when(c == 0)
    def _():
        give_y.wait_recv()

    last.wait_recv()
    sent += list(trade.values()) + [last]
    right = jnp.concatenate([rfull[0], rfull[1]], axis=1)
    surrogate = nn(nt(right, ymat[...]), ymat[...])
    fit_out[...] = nn(surrogate, f_ref[...])
    chaos_out[...] = chaos_scale * surrogate[:, 0 : chaos_out.shape[1]]

    @pl.when(c == 0)
    def _():
        give_p.wait_send()

    @pl.when(c == 1)
    def _():
        give_y.wait_send()

    for copy in sent:
        copy.wait_send()


def main(own, samples, rates_t, order, powers, terms, scale, chaos_scale):
    f32, bf16 = jnp.float32, jnp.bfloat16
    dma = pltpu.SemaphoreType.DMA
    cells, width = samples.shape
    anywhere = pl.BlockSpec(memory_space=pl.ANY)
    square = pltpu.VMEM((TERM_PAD, TERM_PAD), f32)
    return pl.pallas_call(
        functools.partial(main_kernel, scale, chaos_scale),
        out_shape=(
            jax.ShapeDtypeStruct((K, width), f32),
            jax.ShapeDtypeStruct((K, width), f32),
            jax.ShapeDtypeStruct((K, terms), f32),
            jax.ShapeDtypeStruct((K // NY, cells), f32),
        ),
        in_specs=[anywhere] * 2 + [VMEM] * 4,
        out_specs=(VMEM,) * 4,
        scratch_shapes=[
            pltpu.VMEM((NY, K, cells), f32),
            pltpu.VMEM((cells, width), bf16),
            pltpu.VMEM((2 * M, cells), bf16),
            pltpu.VMEM((2 * M, width), f32),
            pltpu.VMEM((2 * K, 2 * M), f32),
            pltpu.VMEM((M, width), f32),
            pltpu.VMEM((K, M), f32),
            square,
            square,
            pltpu.VMEM((8, TERM_PAD), jnp.int32),
            pltpu.VMEM((TERM_PAD, TABLE), bf16),
            pltpu.VMEM((TERM_PAD, TABLE), bf16),
            pltpu.VMEM((TABLE, CHUNK), bf16),
            pltpu.VMEM((TABLE, CHUNK), bf16),
            pltpu.VMEM((PART, CHUNK), f32),
            pltpu.VMEM((NX, M, 128), f32),
            pltpu.VMEM((NX, 8, M), f32),
            pltpu.VMEM((NX, M, 128), f32),
            pltpu.VMEM((NX, 8, M), f32),
            pltpu.VMEM((NX, M, 128), f32),
            pltpu.VMEM((NX, 8, M), f32),
            pltpu.VMEM((NZ, M // NZ, 128), f32),
            pltpu.VMEM((NZ, M // NZ, 128), f32),
            pltpu.VMEM((NZ, 8, M), f32),
            pltpu.VMEM((NZ, M // NZ, 128), f32),
            pltpu.VMEM((NX, 8, M), f32),
            pltpu.VMEM((NY, 2, NX, 8, M), f32),
            square,
            *ELIMINATION,
            pltpu.VMEM((M, M), f32),
            pltpu.VMEM((K, 2 * K), f32),
            pltpu.VMEM((K, K), f32),
            pltpu.VMEM((K, M), f32),
            pltpu.VMEM((TERM_PAD, width), f32),
            pltpu.VMEM((2, NX, K, 128), f32),
            pltpu.VMEM((2, K, 256), f32),
            pltpu.VMEM((NY, K, 256), f32),
            pltpu.VMEM((2, K, 256), f32),
            dma((NY, 2 * PIECES)), dma((NY, 2 * PIECES)),
            dma((2, NX)), dma((2, NX)),
            dma((2, NX)), dma((2, NX)),
            dma((2, NZ)), dma((2, NZ)),
            dma((NZ,)), dma((NZ,)),
            dma((NX,)), dma((NX,)),
            dma((NY,)), dma((NY,)),
            dma((NY,)), dma((NY,)),
            dma((2,)), dma((2,)),
            dma((NX,)), dma((NX,)),
            dma((NX,)), dma((NX,)),
            dma((NY,)), dma((NY,)),
            dma((1,)), dma((1,)),
            dma((2,)),
        ],
        compiler_params=pltpu.CompilerParams(
            collective_id=0, has_side_effects=True, vmem_limit_bytes=60 * 2**20
        ),
        cost_estimate=cost(10**11, 2 * 10**7),
    )(own, samples, rates_t, order, powers, table_codes())


def hand_over_kernel(*refs):
    count = len(refs) // 2
    for src, dst in zip(refs[:count], refs[count:]):
        dst[...] = src[...]


def hand_over(arrays):
    return pl.pallas_call(
        hand_over_kernel,
        out_shape=tuple(jax.ShapeDtypeStruct(a.shape, a.dtype) for a in arrays),
        in_specs=[VMEM] * len(arrays),
        out_specs=(VMEM,) * len(arrays),
    )(*arrays)


def local(snapshots, samples, sample_rates, sample_order, term_powers):
    total, terms = sample_rates.shape[0], term_powers.shape[0]
    cell_count = snapshots.shape[0] * lax.axis_size("space")
    outs = main(
        snapshots.T, samples, sample_rates.T, sample_order[None], term_powers.T,
        terms, math.sqrt(cell_count), math.sqrt(total),
    )
    coeffs, fitted, chaos, pod_modes = hand_over(outs)
    return (pod_modes.T, coeffs.T, fitted.T, chaos.T)


def solution(mesh):
    placed = (P("space", "col"), P("space", "col"), P(), P("col"), P())
    return jax.shard_map(
        local,
        mesh=mesh,
        in_specs=placed,
        out_specs=(P("space", "col"), P("col", None), P("col", None), P()),
        check_vma=False,
    )
```

```python
import functools
import itertools
import math

import jax
import jax.numpy as jnp
import numpy as np
from jax import lax
from jax.experimental import pallas as pl
from jax.experimental.pallas import tpu as pltpu
from jax.sharding import PartitionSpec as P

K = 64
M = 256
SWEEPS = 3
NX, NZ, NY = 4, 8, 4

top_degree = 4
ridge = 0.05

EXACT = lax.Precision.HIGHEST
TERM_PAD = 512
TABLE = 256
PART = 80
CHUNK = 1024
PIECES = 8
BLOCK = 128
MESH = pl.DeviceIdType.MESH
VMEM = pl.BlockSpec(memory_space=pltpu.VMEM)


def nn(a, b, precision=EXACT):
    return lax.dot_general(
        a, b, (((1,), (0,)), ((), ())), precision=precision, preferred_element_type=jnp.float32
    )


def nt(a, b, precision=EXACT):
    return lax.dot_general(
        a, b, (((1,), (1,)), ((), ())), precision=precision, preferred_element_type=jnp.float32
    )


def tn(a, b, precision=EXACT):
    return lax.dot_general(
        a, b, (((0,), (0,)), ((), ())), precision=precision, preferred_element_type=jnp.float32
    )


def cost(flops, bytes_accessed):
    return pl.CostEstimate(flops=flops, bytes_accessed=bytes_accessed, transcendentals=0)


def eye(n):
    rows = lax.broadcasted_iota(jnp.int32, (n, n), 0)
    return (rows == lax.broadcasted_iota(jnp.int32, (n, n), 1)).astype(jnp.float32)


def pivot_block(top, at, w):
    r = [jnp.broadcast_to(top[k : k + 1, :], (8, w)) for k in range(8)]
    a = [
        [jnp.broadcast_to(r[i][:, at + j : at + j + 1], (8, w)) for j in range(i + 1)] for i in range(8)
    ]
    s = [[None] * 8 for _ in range(8)]
    inv = [None] * 8
    for j in range(8):
        inv[j] = lax.rsqrt(a[j][j])
        r[j] = r[j] * inv[j]
        for i in range(j + 1, 8):
            s[i][j] = a[i][j] * inv[j]
        for i in range(j + 1, 8):
            for k in range(j + 1, i + 1):
                a[i][k] = a[i][k] - s[i][j] * s[k][j]
            r[i] = r[i] - s[i][j] * r[j]
    q = [None] * 8
    for k in reversed(range(8)):
        v = r[k]
        for m in reversed(range(k + 1, 8)):
            v = v - s[m][k] * q[m]
        q[k] = v * inv[k]
    return r, q


def merge_rows(r, w):
    sub = lax.broadcasted_iota(jnp.int32, (8, w), 0)
    rows = r[0]
    for k in range(1, 8):
        rows = jnp.where(sub == k, r[k], rows)
    return rows


def inverse_factor(aug, out, n):
    w = 2 * n
    groups = n // 8

    def body(b, carry):
        r, q = pivot_block(aug[0:8, :], 0, w)
        out[pl.ds(pl.multiple_of(8 * b, 8), 8), :] = pltpu.roll(merge_rows(r, w), 8 * b + n, 1)[:, :n]
        rest = aug[8:n, :].reshape(groups - 1, 8, w)
        upd = rest
        for k in range(8):
            upd = upd - jnp.broadcast_to(rest[:, :, k : k + 1], rest.shape) * q[k][None]
        aug[0 : n - 8, :] = pltpu.roll(upd.reshape(n - 8, w), w - 8, 1)
        return carry

    lax.fori_loop(0, groups, body, 0)


def pivot_values(top, at):
    r = [[jnp.broadcast_to(piece[k : k + 1, :], (8, 128)) for piece in top] for k in range(8)]
    a = [
        [jnp.broadcast_to(r[i][0][:, at + j : at + j + 1], (8, 128)) for j in range(i + 1)]
        for i in range(8)
    ]
    low = [[None] * 8 for _ in range(8)]
    q = [None] * 8
    for j in range(8):
        inv = lax.rsqrt(a[j][j])
        r[j] = [v * inv for v in r[j]]
        for k in range(j):
            low[j][k] = low[j][k] * inv
        low[j][j] = inv
        for k in range(j + 1):
            term = [low[j][k] * v for v in r[j]]
            q[k] = term if k == j else [u + v for u, v in zip(q[k], term)]
        s = {i: a[i][j] * inv for i in range(j + 1, 8)}
        for i in range(j + 1, 8):
            for k in range(j + 1, i + 1):
                a[i][k] = a[i][k] - s[i] * s[k]
        for i in range(j + 1, 8):
            r[i] = [u - s[i] * v for u, v in zip(r[i], r[j])]
            for k in range(j + 1):
                step = s[i] * low[j][k]
                low[i][k] = -step if low[i][k] is None else low[i][k] - step
    return r, q


def merge_values(r):
    sub = lax.broadcasted_iota(jnp.int32, (8, 128), 0)
    pieces = []
    for p in range(len(r[0])):
        rows = r[0][p]
        for k in range(1, 8):
            rows = jnp.where(sub == k, r[k][p], rows)
        pieces.append(rows)
    return jnp.concatenate(pieces, axis=1) if len(pieces) > 1 else pieces[0]


def pod_factor(m, aug, cinv):
    full = jnp.concatenate([m, eye(K)], axis=1)
    rows = [full[8 * i : 8 * i + 8, :] for i in range(K // 8)]
    for b in range(K // 8):
        r, q = pivot_values([rows[b]], 8 * b)
        cinv[8 * b : 8 * b + 8, :] = merge_values(r)[:, K:]
        for i in range(b + 1, K // 8):
            v = rows[i]
            for k in reversed(range(8)):
                at = 8 * b + k
                v = v - jnp.broadcast_to(rows[i][:, at : at + 1], (8, 128)) * q[k][0]
            rows[i] = v
    return cinv[...]


def pod_sweep(last, gram, zbuf, aug, cinv):
    z = zbuf[...]
    w = nn(z, gram[...])
    c = pod_factor(nt(z, w), aug, cinv)
    zbuf[...] = nn(c, z if last else w)


def combos():
    return [c for c in itertools.product(range(top_degree + 1), repeat=4) if sum(c) <= top_degree]


def table_codes():
    column = np.full((TABLE, 1), -1, np.int32)
    for m, c in enumerate(combos()):
        for part in range(3):
            column[PART * part + m] = sum(e * 5**i for i, e in enumerate(c))
    return jnp.asarray(column)


def selector(powers, codes):
    code = powers[0:1, :]
    for i in range(1, 4):
        code = code + powers[i : i + 1, :] * 5**i
    return jnp.where(codes == code, 1.0, 0.0).T.astype(jnp.bfloat16)


def fill_table(levels, first, parts, table):
    for m, c in enumerate(combos()):
        row = None
        for i, e in enumerate(c):
            if e:
                level = levels[e][first + i : first + i + 1, :]
                row = level if row is None else row * level
        table[m : m + 1, :] = jnp.ones_like(levels[1][0:1, :]) if row is None else row
    full = table[...]
    high = full.astype(jnp.bfloat16)
    left = full - high.astype(jnp.float32)
    mid = left.astype(jnp.bfloat16)
    parts[0:PART, :] = high
    parts[PART : 2 * PART, :] = mid
    parts[2 * PART : 3 * PART, :] = (left - mid.astype(jnp.float32)).astype(jnp.bfloat16)


def features(points, sa, sb, ta, tb, table):
    he = [jnp.ones_like(points), points]
    for d in range(1, top_degree):
        he.append(points * he[d] - d * he[d - 1])
    levels = [he[d] / math.sqrt(math.factorial(d)) for d in range(top_degree + 1)]
    fill_table(levels, 0, ta, table)
    fill_table(levels, 4, tb, table)
    return nn(sa[...], ta[...], None) * nn(sb[...], tb[...], None)


def picked_points(rates, order):
    total, width = rates.shape[1], order.shape[1]
    high = rates.astype(jnp.bfloat16).astype(jnp.float32)
    left = rates - high
    mid = left.astype(jnp.bfloat16).astype(jnp.float32)
    parts = jnp.concatenate([high, mid, left - mid, jnp.zeros_like(left)], axis=0).astype(jnp.bfloat16)
    piece = 512
    row = lax.broadcasted_iota(jnp.int32, (piece, width), 0)
    found = jnp.zeros((32, width), jnp.float32)
    for at in range(0, total, piece):
        hit = jnp.where(row == order - at, 1.0, 0.0).astype(jnp.bfloat16)
        found = found + nn(parts[:, at : at + piece], hit, None)
    return (found[0:8] + found[8:16]) + found[16:24]


def inverse_block(lo, amat, ymat, aug, linv):
    hi = lo + BLOCK
    aug[...] = jnp.concatenate([amat[lo:hi, lo:hi], eye(BLOCK)], axis=1)
    inverse_factor(aug, linv, BLOCK)
    li = linv[...]
    if lo:
        ymat[lo:hi, 0:lo] = nn(li, ymat[lo:hi, 0:lo])
    ymat[lo:hi, lo:hi] = li
    if hi < TERM_PAD:
        panel = nt(amat[hi:, lo:hi], li)
        amat[hi:, hi:] = amat[hi:, hi:] - nt(panel, panel)
        ymat[hi:, 0:hi] = ymat[hi:, 0:hi] - nn(panel, ymat[lo:hi, 0:hi])


ELIMINATION = [
    pltpu.VMEM((BLOCK, 2 * BLOCK), jnp.float32),
    pltpu.VMEM((BLOCK, BLOCK), jnp.float32),
]


def split(x):
    high = x.astype(jnp.bfloat16)
    return high, (x - high.astype(jnp.float32)).astype(jnp.bfloat16)


def gram_product(first, piece, slots, shards, parts_ref, gacc):
    both = jnp.concatenate([half for e in range(NY) for half in split(shards[slots[e], :, piece])], axis=0)
    parts_ref[:, piece] = both
    gram = nt(both[0 : 2 * K], both, None)
    gacc[...] = gram if first else gacc[...] + gram


def sample_product(first, piece, samples_ref, parts_ref, acc):
    out = nn(parts_ref[:, piece], samples_ref[piece, :], None)
    acc[...] = out if first else acc[...] + out


def place():
    s = lax.axis_index("space")
    return s // (NZ * 2), (s // 2) % NZ, s % 2, lax.axis_index("col")


def device(x, z, c, y):
    return {"space": (x * NZ + z) * 2 + c, "col": y}


def send(src, dst, send_sem, recv_sem, peer):
    copy = pltpu.make_async_remote_copy(
        src_ref=src,
        dst_ref=dst,
        send_sem=send_sem,
        recv_sem=recv_sem,
        device_id=peer,
        device_id_type=MESH,
    )
    copy.start()
    return copy


def lanes(k):
    return pl.ds(pl.multiple_of(k * 128, 128), 128)


def main_kernel(
    scale, chaos_scale,
    own_hbm, samples_hbm, rates_ref, order_ref, powers_ref, codes_ref,
    mc_out, fit_out, chaos_out, pod_out,
    shards, samples_ref, parts_ref, acc, gacc, w_ref, g_ref,
    hh, hl, powers, sa, sb, ta, tb, table,
    cw, cg, sxw, sxg, rxw, rxg, xw, zw, zg, wfull, gx, gfull,
    ymat, aug, linv, gram, aug_p, cinv, pbuf, f_ref,
    mall, half, ry, rfull,
    s_ag, r_ag, s_gp, r_gp,
    s_c, r_c, s_x, r_x, s_z, r_z, s_wz, r_wz, s_gx, r_gx, s_gy, r_gy, s_gc, r_gc,
    s_swap, r_swap, s_mx, r_mx, s_mc, r_mc, s_y, r_y, s_p, r_p, load,
):
    x, z, c, y = place()
    xs = [lax.rem(x + d, NX) for d in range(NX)]
    zs = [lax.rem(z + d, NZ) for d in range(NZ)]
    ys = [lax.rem(y + d, NY) for d in range(NY)]
    partner = device(x, z, 1 - c, y)
    x_peers = [device(xs[d], z, c, y) for d in range(NX)]
    z_peers = [device(x, zs[d], c, y) for d in range(NZ)]
    y_peers = [device(x, z, c, ys[d]) for d in range(NY)]
    x_order, z_order, y_order = (2, 1, 3, 0), (4, 3, 5, 2, 6, 1, 7), (2, 1, 3)
    loads = [
        pltpu.make_async_copy(own_hbm, shards.at[0], load.at[0]),
        pltpu.make_async_copy(samples_hbm, samples_ref, load.at[1]),
    ]
    for copy in loads:
        copy.start()
    peers = y_peers[1:] + [partner] + x_peers[1:] + z_peers[1:]
    barrier = pltpu.get_barrier_semaphore()
    for peer in peers:
        pl.semaphore_signal(barrier, inc=1, device_id=peer, device_id_type=MESH)
    for ref in (hh, hl, ymat, ta, tb, table):
        ref[...] = jnp.zeros_like(ref)
    powers[...] = jnp.full_like(powers, -1)
    powers[:, 0 : powers_ref.shape[1]] = powers_ref[...]
    pl.semaphore_wait(barrier, len(peers))
    sent = []

    top, bottom = pl.ds(0, K // 2), pl.ds(K // 2, K // 2)
    cells = samples_ref.shape[0]
    pieces = [pl.ds(at, cells // PIECES) for at in range(0, cells, cells // PIECES)]
    near = {}
    for i, piece in enumerate(pieces):
        for d in (3, 1):
            slot = NY - d
            near[d, i] = send(
                own_hbm.at[:, piece], shards.at[slot, :, piece], s_ag.at[d, i], r_ag.at[slot, i], y_peers[d]
            )
            sent.append(near[d, i])
    far = {}

    def relay(i):
        for h, (d, src, part) in enumerate(((3, 1, top), (1, 3, bottom))):
            near[d, i].wait_recv()
            far[h, i] = send(
                shards.at[src, part, pieces[i]], shards.at[2, part, pieces[i]],
                s_ag.at[2 * h, PIECES + i], r_ag.at[2 * h, PIECES + i], y_peers[d],
            )
            sent.append(far[h, i])

    sa[...] = selector(powers[0:4, :], codes_ref[...])
    sb[...] = selector(powers[4:8, :], codes_ref[...])
    total = rates_ref.shape[1]

    def chunk(step, carry):
        v = rates_ref[:, pl.ds(pl.multiple_of(step * CHUNK, CHUNK), CHUNK)]
        high, low = split(features(v, sa, sb, ta, tb, table))
        hh[...] += nt(high, high, None)
        hl[...] += nt(high, low, None)
        return carry

    lax.fori_loop(0, total // CHUNK, chunk, 0)
    for i in range(4):
        relay(i)
    f_ref[...] = features(picked_points(rates_ref[...], order_ref[...]), sa, sb, ta, tb, table)
    amat = hh
    amat[...] = hh[...] + hl[...] + hl[...].T + (ridge * total) * eye(TERM_PAD)
    inverse_block(0, amat, ymat, aug, linv)
    relay(4)
    relay(5)
    inverse_block(BLOCK, amat, ymat, aug, linv)
    relay(6)
    relay(7)

    for copy in loads:
        copy.wait()
    slots = (0, 1, 3, 2)
    for i, piece in enumerate(pieces):
        far[0, i].wait_recv()
        far[1, i].wait_recv()
        gram_product(i == 0, piece, slots, shards, parts_ref, gacc)
        if i < PIECES - 1:
            sample_product(i == 0, piece, samples_ref, parts_ref, acc)
    grams = gacc[0:K, :] + gacc[K:, :]
    blocks = [grams[:, 2 * K * e : 2 * K * e + K] + grams[:, 2 * K * e + K : 2 * K * (e + 1)] for e in (0, 1, 3, 2)]
    g_ref[...] = pltpu.roll(jnp.concatenate(blocks, axis=1), y * K, 1).reshape(g_ref.shape)
    early = send(g_ref.at[1 - c], cg, s_gp.at[0], r_gp.at[0], partner)
    sent.append(early)

    sample_product(False, pieces[-1], samples_ref, parts_ref, acc)
    early.wait_recv()
    second = {}
    for d in x_order:
        gsum = g_ref[c, xs[d]] + cg[xs[d]]
        if d:
            sxg[d] = gsum
            second[d] = [send(sxg.at[d], rxg.at[x], s_x.at[0, d], r_x.at[0, d], x_peers[d])]
        else:
            rxg[pl.ds(x, 1)] = gsum[None]
    for e in range(NY):
        row = pl.multiple_of(ys[slots[e]] * K, K)
        lo = 2 * K * e
        w_ref[pl.ds(row, K), :] = acc[lo : lo + K, :] + acc[lo + K : lo + 2 * K, :]

    first = {}
    for d in x_order:
        other = (1 - c) * NX + xs[d]
        first[d] = send(w_ref.at[:, lanes(other)], cw.at[d], s_c.at[d], r_c.at[d], partner)
        sent.append(first[d])
    for d in x_order:
        first[d].wait_recv()
        wsum = w_ref[:, lanes(c * NX + xs[d])] + cw[d]
        if d:
            sxw[d] = wsum
            second[d].append(send(sxw.at[d], rxw.at[x], s_x.at[1, d], r_x.at[1, d], x_peers[d]))
            sent += second[d]
        else:
            rxw[pl.ds(x, 1)] = wsum[None]

    for d in (1, 3, 2):
        second[d][0].wait_recv()
    sxg[0] = ((rxg[0] + rxg[1]) + rxg[2]) + rxg[3]
    zg[pl.ds(z, 1)] = sxg[0][None]
    third = {}
    for d in z_order:
        third[d] = [send(sxg.at[0], zg.at[z], s_z.at[0, d], r_z.at[0, d], z_peers[d])]
    for d in z_order:
        third[d][0].wait_recv()
    total = zg[0]
    for k in range(1, NZ):
        total = total + zg[k]
    gx[pl.ds(x, 1)] = total[None]
    fourth = {}
    for d in (2, 1, 3):
        fourth[d] = send(gx.at[x], gx.at[x], s_gx.at[d], r_gx.at[d], x_peers[d])
        sent.append(fourth[d])

    for d in (1, 3, 2):
        second[d][1].wait_recv()
    xw[...] = (((rxw[0] + rxw[1]) + rxw[2]) + rxw[3]).reshape(xw.shape)
    for d in z_order:
        third[d].append(send(xw.at[zs[d]], zw.at[z], s_z.at[1, d], r_z.at[1, d], z_peers[d]))
        sent += third[d]
    zw[pl.ds(z, 1)] = xw[pl.ds(z, 1)]

    for d in (1, 3, 2):
        fourth[d].wait_recv()
    gfull[pl.ds(y, 1), pl.ds(c, 1)] = gx[...][None, None]
    sixth = {}
    for d in y_order:
        sixth[d] = send(gx, gfull.at[y, c], s_gy.at[d], r_gy.at[d], y_peers[d])
        sent.append(sixth[d])
    seventh = [send(gx, gfull.at[y, c], s_gc.at[0], r_gc.at[0], partner)]
    for d in (1, 3, 2):
        sixth[d].wait_recv()
        src = lax.rem(y + NY - d, NY)
        seventh.append(send(gfull.at[src, c], gfull.at[src, c], s_gc.at[d], r_gc.at[d], partner))
    sent += seventh
    for copy in seventh:
        copy.wait_recv()

    tail = pl.ds(TERM_PAD - 2 * BLOCK, 2 * BLOCK)
    give_p = pltpu.make_async_remote_copy(
        src_ref=pbuf, dst_ref=pbuf, send_sem=s_swap.at[0], recv_sem=r_swap.at[0],
        device_id=partner, device_id_type=MESH,
    )
    give_y = pltpu.make_async_remote_copy(
        src_ref=ymat.at[tail, :], dst_ref=ymat.at[tail, :], send_sem=s_swap.at[1], recv_sem=r_swap.at[1],
        device_id=partner, device_id_type=MESH,
    )

    @pl.when(c == 0)
    def _():
        for k in range(NY):
            gram[K * k : K * k + K, :] = gfull[k].reshape(K, M)
        pbuf[...] = nn(pod_factor(gram[0:K, 0:K], aug_p, cinv), gram[0:K, :])
        pod_sweep(False, gram, pbuf, aug_p, cinv)

    @pl.when(c == 1)
    def _():
        inverse_block(2 * BLOCK, amat, ymat, aug, linv)

    for d in z_order:
        third[d][1].wait_recv()
    total = zw[0]
    for k in range(1, NZ):
        total = total + zw[k]
    wfull[pl.ds(z, 1)] = total[None]
    fifth = {}
    for d in z_order:
        fifth[d] = send(wfull.at[z], wfull.at[z], s_wz.at[d], r_wz.at[d], z_peers[d])
        sent.append(fifth[d])

    @pl.when(c == 0)
    def _():
        pod_sweep(False, gram, pbuf, aug_p, cinv)
        pod_sweep(True, gram, pbuf, aug_p, cinv)
        give_p.start()

    @pl.when(c == 1)
    def _():
        inverse_block(3 * BLOCK, amat, ymat, aug, linv)
        give_y.start()
        give_p.wait_recv()

    for d in z_order:
        fifth[d].wait_recv()
    p = pbuf[...]
    mine = mall.at[c, x]
    mall[pl.ds(c, 1), pl.ds(x, 1)] = nn(p, wfull[...].reshape(M, 128))[None, None]
    swaps = [send(mine, mine, s_mc.at[0], r_mc.at[0], partner)]
    moves = {}
    for d in (2, 1, 3):
        moves[d] = send(mine, mine, s_mx.at[d], r_mx.at[d], x_peers[d])
    for d in (1, 3, 2):
        moves[d].wait_recv()
        src = mall.at[c, lax.rem(x + NX - d, NX)]
        swaps.append(send(src, src, s_mc.at[d], r_mc.at[d], partner))
    for copy in swaps:
        copy.wait_recv()
    sent += swaps + list(moves.values())
    coeffs = jnp.concatenate([mall[k // NX, k % NX] for k in range(2 * NX)], axis=1)
    part = nt(coeffs, f_ref[...])
    half[...] = jnp.concatenate([part[:, 0:256], part[:, 256:]], axis=0).reshape(half.shape)
    rows = half.at[c]
    ry[pl.ds(y, 1)] = half[pl.ds(c, 1)]
    trade = {}
    for d in (2, 1, 3):
        trade[d] = send(rows, ry.at[y], s_y.at[d], r_y.at[d], y_peers[d])
    mc_out[...] = coeffs

    width = pod_out.shape[0]
    shift = lax.rem(NY - y, NY) * K
    picked = pltpu.roll(pbuf[pl.ds(pl.multiple_of(y * width, width), width), :] * scale, shift, 1)
    cuts = [picked[:, K * d : K * d + K] for d in slots]
    picked = jnp.concatenate([cuts[e // 2] for e in range(2 * NY)], axis=1)
    outer = nn(jnp.concatenate(split(picked), axis=0), parts_ref[...], None)
    pod_out[...] = outer[0:width] + outer[width:]

    for d in (1, 3, 2):
        trade[d].wait_recv()
    rfull[pl.ds(c, 1)] = (((ry[0] + ry[1]) + ry[2]) + ry[3])[None]
    last = send(rfull.at[c], rfull.at[c], s_p.at[0], r_p.at[0], partner)

    @pl.when(c == 0)
    def _():
        give_y.wait_recv()

    last.wait_recv()
    sent += list(trade.values()) + [last]
    right = jnp.concatenate([rfull[0], rfull[1]], axis=1)
    surrogate = nn(nt(right, ymat[...]), ymat[...])
    fit_out[...] = nn(surrogate, f_ref[...])
    chaos_out[...] = chaos_scale * surrogate[:, 0 : chaos_out.shape[1]]

    @pl.when(c == 0)
    def _():
        give_p.wait_send()

    @pl.when(c == 1)
    def _():
        give_y.wait_send()

    for copy in sent:
        copy.wait_send()


def main(own, samples, rates_t, order, powers, terms, scale, chaos_scale):
    f32, bf16 = jnp.float32, jnp.bfloat16
    dma = pltpu.SemaphoreType.DMA
    cells, width = samples.shape
    anywhere = pl.BlockSpec(memory_space=pl.ANY)
    square = pltpu.VMEM((TERM_PAD, TERM_PAD), f32)
    return pl.pallas_call(
        functools.partial(main_kernel, scale, chaos_scale),
        out_shape=(
            jax.ShapeDtypeStruct((K, width), f32),
            jax.ShapeDtypeStruct((K, width), f32),
            jax.ShapeDtypeStruct((K, terms), f32),
            jax.ShapeDtypeStruct((K // NY, cells), f32),
        ),
        in_specs=[anywhere] * 2 + [VMEM] * 4,
        out_specs=(VMEM,) * 4,
        scratch_shapes=[
            pltpu.VMEM((NY, K, cells), f32),
            pltpu.VMEM((cells, width), bf16),
            pltpu.VMEM((2 * M, cells), bf16),
            pltpu.VMEM((2 * M, width), f32),
            pltpu.VMEM((2 * K, 2 * M), f32),
            pltpu.VMEM((M, width), f32),
            pltpu.VMEM((2, NX, 8, M), f32),
            square,
            square,
            pltpu.VMEM((8, TERM_PAD), jnp.int32),
            pltpu.VMEM((TERM_PAD, TABLE), bf16),
            pltpu.VMEM((TERM_PAD, TABLE), bf16),
            pltpu.VMEM((TABLE, CHUNK), bf16),
            pltpu.VMEM((TABLE, CHUNK), bf16),
            pltpu.VMEM((PART, CHUNK), f32),
            pltpu.VMEM((NX, M, 128), f32),
            pltpu.VMEM((NX, 8, M), f32),
            pltpu.VMEM((NX, M, 128), f32),
            pltpu.VMEM((NX, 8, M), f32),
            pltpu.VMEM((NX, M, 128), f32),
            pltpu.VMEM((NX, 8, M), f32),
            pltpu.VMEM((NZ, M // NZ, 128), f32),
            pltpu.VMEM((NZ, M // NZ, 128), f32),
            pltpu.VMEM((NZ, 8, M), f32),
            pltpu.VMEM((NZ, M // NZ, 128), f32),
            pltpu.VMEM((NX, 8, M), f32),
            pltpu.VMEM((NY, 2, NX, 8, M), f32),
            square,
            *ELIMINATION,
            pltpu.VMEM((M, M), f32),
            pltpu.VMEM((K, 2 * K), f32),
            pltpu.VMEM((K, K), f32),
            pltpu.VMEM((K, M), f32),
            pltpu.VMEM((TERM_PAD, width), f32),
            pltpu.VMEM((2, NX, K, 128), f32),
            pltpu.VMEM((2, K, 256), f32),
            pltpu.VMEM((NY, K, 256), f32),
            pltpu.VMEM((2, K, 256), f32),
            dma((NY, 2 * PIECES)), dma((NY, 2 * PIECES)), dma((1,)), dma((1,)),
            dma((NX,)), dma((NX,)),
            dma((2, NX)), dma((2, NX)),
            dma((2, NZ)), dma((2, NZ)),
            dma((NZ,)), dma((NZ,)),
            dma((NX,)), dma((NX,)),
            dma((NY,)), dma((NY,)),
            dma((NY,)), dma((NY,)),
            dma((2,)), dma((2,)),
            dma((NX,)), dma((NX,)),
            dma((NX,)), dma((NX,)),
            dma((NY,)), dma((NY,)),
            dma((1,)), dma((1,)),
            dma((2,)),
        ],
        compiler_params=pltpu.CompilerParams(
            collective_id=0, has_side_effects=True, vmem_limit_bytes=60 * 2**20
        ),
        cost_estimate=cost(10**11, 2 * 10**7),
    )(own, samples, rates_t, order, powers, table_codes())


def hand_over_kernel(*refs):
    count = len(refs) // 2
    for src, dst in zip(refs[:count], refs[count:]):
        dst[...] = src[...]


def hand_over(arrays):
    return pl.pallas_call(
        hand_over_kernel,
        out_shape=tuple(jax.ShapeDtypeStruct(a.shape, a.dtype) for a in arrays),
        in_specs=[VMEM] * len(arrays),
        out_specs=(VMEM,) * len(arrays),
    )(*arrays)


def local(snapshots, samples, sample_rates, sample_order, term_powers):
    total, terms = sample_rates.shape[0], term_powers.shape[0]
    cell_count = snapshots.shape[0] * lax.axis_size("space")
    outs = main(
        snapshots.T, samples, sample_rates.T, sample_order[None], term_powers.T,
        terms, math.sqrt(cell_count), math.sqrt(total),
    )
    coeffs, fitted, chaos, pod_modes = hand_over(outs)
    return (pod_modes.T, coeffs.T, fitted.T, chaos.T)


def solution(mesh):
    placed = (P("space", "col"), P("space", "col"), P(), P("col"), P())
    return jax.shard_map(
        local,
        mesh=mesh,
        in_specs=placed,
        out_specs=(P("space", "col"), P("col", None), P("col", None), P()),
        check_vma=False,
    )
```

```python
import functools
import itertools
import math

import jax
import jax.numpy as jnp
import numpy as np
from jax import lax
from jax.experimental import pallas as pl
from jax.experimental.pallas import tpu as pltpu
from jax.sharding import PartitionSpec as P

K = 64
M = 256
SWEEPS = 3
NX, NZ, NY = 4, 8, 4

top_degree = 4
ridge = 0.05

EXACT = lax.Precision.HIGHEST
TERM_PAD = 512
TABLE = 256
PART = 80
CHUNK = 1024
PIECES = 8
BLOCK = 128
MESH = pl.DeviceIdType.MESH
VMEM = pl.BlockSpec(memory_space=pltpu.VMEM)


def nn(a, b, precision=EXACT):
    return lax.dot_general(
        a, b, (((1,), (0,)), ((), ())), precision=precision, preferred_element_type=jnp.float32
    )


def nt(a, b, precision=EXACT):
    return lax.dot_general(
        a, b, (((1,), (1,)), ((), ())), precision=precision, preferred_element_type=jnp.float32
    )


def tn(a, b, precision=EXACT):
    return lax.dot_general(
        a, b, (((0,), (0,)), ((), ())), precision=precision, preferred_element_type=jnp.float32
    )


def cost(flops, bytes_accessed):
    return pl.CostEstimate(flops=flops, bytes_accessed=bytes_accessed, transcendentals=0)


def eye(n):
    rows = lax.broadcasted_iota(jnp.int32, (n, n), 0)
    return (rows == lax.broadcasted_iota(jnp.int32, (n, n), 1)).astype(jnp.float32)


def pivot_block(top, at, w):
    r = [jnp.broadcast_to(top[k : k + 1, :], (8, w)) for k in range(8)]
    a = [
        [jnp.broadcast_to(r[i][:, at + j : at + j + 1], (8, w)) for j in range(i + 1)] for i in range(8)
    ]
    s = [[None] * 8 for _ in range(8)]
    inv = [None] * 8
    for j in range(8):
        inv[j] = lax.rsqrt(a[j][j])
        r[j] = r[j] * inv[j]
        for i in range(j + 1, 8):
            s[i][j] = a[i][j] * inv[j]
        for i in range(j + 1, 8):
            for k in range(j + 1, i + 1):
                a[i][k] = a[i][k] - s[i][j] * s[k][j]
            r[i] = r[i] - s[i][j] * r[j]
    q = [None] * 8
    for k in reversed(range(8)):
        v = r[k]
        for m in reversed(range(k + 1, 8)):
            v = v - s[m][k] * q[m]
        q[k] = v * inv[k]
    return r, q


def merge_rows(r, w):
    sub = lax.broadcasted_iota(jnp.int32, (8, w), 0)
    rows = r[0]
    for k in range(1, 8):
        rows = jnp.where(sub == k, r[k], rows)
    return rows


def inverse_factor(aug, out, n):
    w = 2 * n
    groups = n // 8

    def body(b, carry):
        r, q = pivot_block(aug[0:8, :], 0, w)
        out[pl.ds(pl.multiple_of(8 * b, 8), 8), :] = pltpu.roll(merge_rows(r, w), 8 * b + n, 1)[:, :n]
        rest = aug[8:n, :].reshape(groups - 1, 8, w)
        upd = rest
        for k in range(8):
            upd = upd - jnp.broadcast_to(rest[:, :, k : k + 1], rest.shape) * q[k][None]
        aug[0 : n - 8, :] = pltpu.roll(upd.reshape(n - 8, w), w - 8, 1)
        return carry

    lax.fori_loop(0, groups, body, 0)


def pivot_values(top, at):
    r = [[jnp.broadcast_to(piece[k : k + 1, :], (8, 128)) for piece in top] for k in range(8)]
    a = [
        [jnp.broadcast_to(r[i][0][:, at + j : at + j + 1], (8, 128)) for j in range(i + 1)]
        for i in range(8)
    ]
    low = [[None] * 8 for _ in range(8)]
    q = [None] * 8
    for j in range(8):
        inv = lax.rsqrt(a[j][j])
        r[j] = [v * inv for v in r[j]]
        for k in range(j):
            low[j][k] = low[j][k] * inv
        low[j][j] = inv
        for k in range(j + 1):
            term = [low[j][k] * v for v in r[j]]
            q[k] = term if k == j else [u + v for u, v in zip(q[k], term)]
        s = {i: a[i][j] * inv for i in range(j + 1, 8)}
        for i in range(j + 1, 8):
            for k in range(j + 1, i + 1):
                a[i][k] = a[i][k] - s[i] * s[k]
        for i in range(j + 1, 8):
            r[i] = [u - s[i] * v for u, v in zip(r[i], r[j])]
            for k in range(j + 1):
                step = s[i] * low[j][k]
                low[i][k] = -step if low[i][k] is None else low[i][k] - step
    return r, q


def merge_values(r):
    sub = lax.broadcasted_iota(jnp.int32, (8, 128), 0)
    pieces = []
    for p in range(len(r[0])):
        rows = r[0][p]
        for k in range(1, 8):
            rows = jnp.where(sub == k, r[k][p], rows)
        pieces.append(rows)
    return jnp.concatenate(pieces, axis=1) if len(pieces) > 1 else pieces[0]


def pod_factor(m, aug, cinv):
    full = jnp.concatenate([m, eye(K)], axis=1)
    rows = [full[8 * i : 8 * i + 8, :] for i in range(K // 8)]
    for b in range(K // 8):
        r, q = pivot_values([rows[b]], 8 * b)
        cinv[8 * b : 8 * b + 8, :] = merge_values(r)[:, K:]
        for i in range(b + 1, K // 8):
            v = rows[i]
            for k in reversed(range(8)):
                at = 8 * b + k
                v = v - jnp.broadcast_to(rows[i][:, at : at + 1], (8, 128)) * q[k][0]
            rows[i] = v
    return cinv[...]


def pod_sweep(last, gram, zbuf, aug, cinv):
    z = zbuf[...]
    w = nn(z, gram[...])
    c = pod_factor(nt(z, w), aug, cinv)
    zbuf[...] = nn(c, z if last else w)


def combos():
    return [c for c in itertools.product(range(top_degree + 1), repeat=4) if sum(c) <= top_degree]


def table_codes():
    column = np.full((TABLE, 1), -1, np.int32)
    for m, c in enumerate(combos()):
        for part in range(3):
            column[PART * part + m] = sum(e * 5**i for i, e in enumerate(c))
    return jnp.asarray(column)


def selector(powers, codes):
    code = powers[0:1, :]
    for i in range(1, 4):
        code = code + powers[i : i + 1, :] * 5**i
    return jnp.where(codes == code, 1.0, 0.0).T.astype(jnp.bfloat16)


def fill_table(levels, first, parts, table):
    for m, c in enumerate(combos()):
        row = None
        for i, e in enumerate(c):
            if e:
                level = levels[e][first + i : first + i + 1, :]
                row = level if row is None else row * level
        table[m : m + 1, :] = jnp.ones_like(levels[1][0:1, :]) if row is None else row
    full = table[...]
    high = full.astype(jnp.bfloat16)
    left = full - high.astype(jnp.float32)
    mid = left.astype(jnp.bfloat16)
    parts[0:PART, :] = high
    parts[PART : 2 * PART, :] = mid
    parts[2 * PART : 3 * PART, :] = (left - mid.astype(jnp.float32)).astype(jnp.bfloat16)


def features(points, sa, sb, ta, tb, table):
    he = [jnp.ones_like(points), points]
    for d in range(1, top_degree):
        he.append(points * he[d] - d * he[d - 1])
    levels = [he[d] / math.sqrt(math.factorial(d)) for d in range(top_degree + 1)]
    fill_table(levels, 0, ta, table)
    fill_table(levels, 4, tb, table)
    return nn(sa[...], ta[...], None) * nn(sb[...], tb[...], None)


def picked_points(rates, order):
    total, width = rates.shape[1], order.shape[1]
    high = rates.astype(jnp.bfloat16).astype(jnp.float32)
    left = rates - high
    mid = left.astype(jnp.bfloat16).astype(jnp.float32)
    parts = jnp.concatenate([high, mid, left - mid, jnp.zeros_like(left)], axis=0).astype(jnp.bfloat16)
    piece = 512
    row = lax.broadcasted_iota(jnp.int32, (piece, width), 0)
    found = jnp.zeros((32, width), jnp.float32)
    for at in range(0, total, piece):
        hit = jnp.where(row == order - at, 1.0, 0.0).astype(jnp.bfloat16)
        found = found + nn(parts[:, at : at + piece], hit, None)
    return (found[0:8] + found[8:16]) + found[16:24]


def inverse_block(lo, amat, ymat, aug, linv):
    hi = lo + BLOCK
    aug[...] = jnp.concatenate([amat[lo:hi, lo:hi], eye(BLOCK)], axis=1)
    inverse_factor(aug, linv, BLOCK)
    li = linv[...]
    if lo:
        ymat[lo:hi, 0:lo] = nn(li, ymat[lo:hi, 0:lo])
    ymat[lo:hi, lo:hi] = li
    if hi < TERM_PAD:
        panel = nt(amat[hi:, lo:hi], li)
        amat[hi:, hi:] = amat[hi:, hi:] - nt(panel, panel)
        ymat[hi:, 0:hi] = ymat[hi:, 0:hi] - nn(panel, ymat[lo:hi, 0:hi])


ELIMINATION = [
    pltpu.VMEM((BLOCK, 2 * BLOCK), jnp.float32),
    pltpu.VMEM((BLOCK, BLOCK), jnp.float32),
]


def split(x):
    high = x.astype(jnp.bfloat16)
    return high, (x - high.astype(jnp.float32)).astype(jnp.bfloat16)


def thirds(x):
    high = x.astype(jnp.bfloat16)
    left = x - high.astype(jnp.float32)
    mid = left.astype(jnp.bfloat16)
    return high, mid, (left - mid.astype(jnp.float32)).astype(jnp.bfloat16)


def stacked(dot, x, parts):
    n = x.shape[0]
    high, mid, low = thirds(x)
    a = dot(jnp.concatenate([high, mid, low], axis=0), parts[0], None)
    b = dot(jnp.concatenate([high, mid], axis=0), parts[1], None)
    c = dot(high, parts[2], None)
    return a[0:n] + ((a[n : 2 * n] + b[0:n]) + ((a[2 * n :] + b[n:]) + c))


def gram_product(first, piece, slots, shards, parts_ref, gacc):
    both = jnp.concatenate([half for e in range(NY) for half in split(shards[slots[e], :, piece])], axis=0)
    parts_ref[:, piece] = both
    gram = nt(both[0 : 2 * K], both, None)
    gacc[...] = gram if first else gacc[...] + gram


def sample_product(first, piece, samples_ref, parts_ref, acc):
    out = nn(parts_ref[:, piece], samples_ref[piece, :], None)
    acc[...] = out if first else acc[...] + out


def place():
    s = lax.axis_index("space")
    return s // (NZ * 2), (s // 2) % NZ, s % 2, lax.axis_index("col")


def device(x, z, c, y):
    return {"space": (x * NZ + z) * 2 + c, "col": y}


def send(src, dst, send_sem, recv_sem, peer):
    copy = pltpu.make_async_remote_copy(
        src_ref=src,
        dst_ref=dst,
        send_sem=send_sem,
        recv_sem=recv_sem,
        device_id=peer,
        device_id_type=MESH,
    )
    copy.start()
    return copy


def lanes(k):
    return pl.ds(pl.multiple_of(k * 128, 128), 128)


def main_kernel(
    scale, chaos_scale,
    own_hbm, samples_hbm, rates_ref, order_ref, powers_ref, codes_ref,
    mc_out, fit_out, chaos_out, pod_out,
    shards, samples_ref, parts_ref, acc, gacc, w_ref, g_ref,
    hh, hl, powers, sa, sb, ta, tb, table,
    cw, cg, sxw, sxg, rxw, rxg, xw, zw, zg, wfull, gx, gfull,
    ymat, aug, linv, gram, aug_p, cinv, pbuf, f_ref,
    mall, half, ry, rfull,
    s_ag, r_ag, s_gp, r_gp,
    s_c, r_c, s_x, r_x, s_z, r_z, s_wz, r_wz, s_gx, r_gx, s_gy, r_gy, s_gc, r_gc,
    s_swap, r_swap, s_mx, r_mx, s_mc, r_mc, s_y, r_y, s_p, r_p, load,
):
    x, z, c, y = place()
    xs = [lax.rem(x + d, NX) for d in range(NX)]
    zs = [lax.rem(z + d, NZ) for d in range(NZ)]
    ys = [lax.rem(y + d, NY) for d in range(NY)]
    partner = device(x, z, 1 - c, y)
    x_peers = [device(xs[d], z, c, y) for d in range(NX)]
    z_peers = [device(x, zs[d], c, y) for d in range(NZ)]
    y_peers = [device(x, z, c, ys[d]) for d in range(NY)]
    x_order, z_order, y_order = (2, 1, 3, 0), (4, 3, 5, 2, 6, 1, 7), (2, 1, 3)
    loads = [
        pltpu.make_async_copy(own_hbm, shards.at[0], load.at[0]),
        pltpu.make_async_copy(samples_hbm, samples_ref, load.at[1]),
    ]
    for copy in loads:
        copy.start()
    peers = y_peers[1:] + [partner] + x_peers[1:] + z_peers[1:]
    barrier = pltpu.get_barrier_semaphore()
    for peer in peers:
        pl.semaphore_signal(barrier, inc=1, device_id=peer, device_id_type=MESH)
    for ref in (hh, hl, ymat, ta, tb, table):
        ref[...] = jnp.zeros_like(ref)
    powers[...] = jnp.full_like(powers, -1)
    powers[:, 0 : powers_ref.shape[1]] = powers_ref[...]
    pl.semaphore_wait(barrier, len(peers))
    sent = []

    top, bottom = pl.ds(0, K // 2), pl.ds(K // 2, K // 2)
    cells = samples_ref.shape[0]
    pieces = [pl.ds(at, cells // PIECES) for at in range(0, cells, cells // PIECES)]
    near = {}
    for i, piece in enumerate(pieces):
        for d in (3, 1):
            slot = NY - d
            near[d, i] = send(
                own_hbm.at[:, piece], shards.at[slot, :, piece], s_ag.at[d, i], r_ag.at[slot, i], y_peers[d]
            )
            sent.append(near[d, i])
    far = {}

    def relay(i):
        for h, (d, src, part) in enumerate(((3, 1, top), (1, 3, bottom))):
            near[d, i].wait_recv()
            far[h, i] = send(
                shards.at[src, part, pieces[i]], shards.at[2, part, pieces[i]],
                s_ag.at[2 * h, PIECES + i], r_ag.at[2 * h, PIECES + i], y_peers[d],
            )
            sent.append(far[h, i])

    sa[...] = selector(powers[0:4, :], codes_ref[...])
    sb[...] = selector(powers[4:8, :], codes_ref[...])
    total = rates_ref.shape[1]

    def chunk(step, carry):
        v = rates_ref[:, pl.ds(pl.multiple_of(step * CHUNK, CHUNK), CHUNK)]
        high, low = split(features(v, sa, sb, ta, tb, table))
        hh[...] += nt(high, high, None)
        hl[...] += nt(high, low, None)
        return carry

    lax.fori_loop(0, total // CHUNK, chunk, 0)
    for i in range(4):
        relay(i)
    f_high, f_mid, f_low = thirds(
        features(picked_points(rates_ref[...], order_ref[...]), sa, sb, ta, tb, table)
    )
    f_ref[0] = f_high
    f_ref[1] = f_mid
    f_ref[2] = f_low
    amat = hh
    amat[...] = hh[...] + hl[...] + hl[...].T + (ridge * total) * eye(TERM_PAD)
    inverse_block(0, amat, ymat, aug, linv)
    relay(4)
    relay(5)
    inverse_block(BLOCK, amat, ymat, aug, linv)
    relay(6)
    relay(7)

    for copy in loads:
        copy.wait()
    slots = (0, 1, 3, 2)
    for i, piece in enumerate(pieces):
        far[0, i].wait_recv()
        far[1, i].wait_recv()
        gram_product(i == 0, piece, slots, shards, parts_ref, gacc)
        if i < PIECES - 1:
            sample_product(i == 0, piece, samples_ref, parts_ref, acc)
    grams = gacc[0:K, :] + gacc[K:, :]
    blocks = [grams[:, 2 * K * e : 2 * K * e + K] + grams[:, 2 * K * e + K : 2 * K * (e + 1)] for e in (0, 1, 3, 2)]
    g_ref[...] = pltpu.roll(jnp.concatenate(blocks, axis=1), y * K, 1).reshape(g_ref.shape)
    early = send(g_ref.at[1 - c], cg, s_gp.at[0], r_gp.at[0], partner)
    sent.append(early)

    sample_product(False, pieces[-1], samples_ref, parts_ref, acc)
    early.wait_recv()
    second = {}
    for d in x_order:
        gsum = g_ref[c, xs[d]] + cg[xs[d]]
        if d:
            sxg[d] = gsum
            second[d] = [send(sxg.at[d], rxg.at[x], s_x.at[0, d], r_x.at[0, d], x_peers[d])]
        else:
            rxg[pl.ds(x, 1)] = gsum[None]
    for e in range(NY):
        row = pl.multiple_of(ys[slots[e]] * K, K)
        lo = 2 * K * e
        w_ref[pl.ds(row, K), :] = acc[lo : lo + K, :] + acc[lo + K : lo + 2 * K, :]

    first = {}
    for d in x_order:
        other = (1 - c) * NX + xs[d]
        first[d] = send(w_ref.at[:, lanes(other)], cw.at[d], s_c.at[d], r_c.at[d], partner)
        sent.append(first[d])
    for d in x_order:
        first[d].wait_recv()
        wsum = w_ref[:, lanes(c * NX + xs[d])] + cw[d]
        if d:
            sxw[d] = wsum
            second[d].append(send(sxw.at[d], rxw.at[x], s_x.at[1, d], r_x.at[1, d], x_peers[d]))
            sent += second[d]
        else:
            rxw[pl.ds(x, 1)] = wsum[None]

    for d in (1, 3, 2):
        second[d][0].wait_recv()
    sxg[0] = ((rxg[0] + rxg[1]) + rxg[2]) + rxg[3]
    zg[pl.ds(z, 1)] = sxg[0][None]
    third = {}
    for d in z_order:
        third[d] = [send(sxg.at[0], zg.at[z], s_z.at[0, d], r_z.at[0, d], z_peers[d])]
    for d in z_order:
        third[d][0].wait_recv()
    total = zg[0]
    for k in range(1, NZ):
        total = total + zg[k]
    gx[pl.ds(x, 1)] = total[None]
    fourth = {}
    for d in (2, 1, 3):
        fourth[d] = send(gx.at[x], gx.at[x], s_gx.at[d], r_gx.at[d], x_peers[d])
        sent.append(fourth[d])

    for d in (1, 3, 2):
        second[d][1].wait_recv()
    xw[...] = (((rxw[0] + rxw[1]) + rxw[2]) + rxw[3]).reshape(xw.shape)
    for d in z_order:
        third[d].append(send(xw.at[zs[d]], zw.at[z], s_z.at[1, d], r_z.at[1, d], z_peers[d]))
        sent += third[d]
    zw[pl.ds(z, 1)] = xw[pl.ds(z, 1)]

    for d in (1, 3, 2):
        fourth[d].wait_recv()
    gfull[pl.ds(y, 1), pl.ds(c, 1)] = gx[...][None, None]
    sixth = {}
    for d in y_order:
        sixth[d] = send(gx, gfull.at[y, c], s_gy.at[d], r_gy.at[d], y_peers[d])
        sent.append(sixth[d])
    seventh = [send(gx, gfull.at[y, c], s_gc.at[0], r_gc.at[0], partner)]
    for d in (1, 3, 2):
        sixth[d].wait_recv()
        src = lax.rem(y + NY - d, NY)
        seventh.append(send(gfull.at[src, c], gfull.at[src, c], s_gc.at[d], r_gc.at[d], partner))
    sent += seventh
    for copy in seventh:
        copy.wait_recv()

    tail = pl.ds(TERM_PAD - 2 * BLOCK, 2 * BLOCK)
    give_p = pltpu.make_async_remote_copy(
        src_ref=pbuf, dst_ref=pbuf, send_sem=s_swap.at[0], recv_sem=r_swap.at[0],
        device_id=partner, device_id_type=MESH,
    )
    give_y = pltpu.make_async_remote_copy(
        src_ref=ymat.at[tail, :], dst_ref=ymat.at[tail, :], send_sem=s_swap.at[1], recv_sem=r_swap.at[1],
        device_id=partner, device_id_type=MESH,
    )

    @pl.when(c == 0)
    def _():
        for k in range(NY):
            gram[K * k : K * k + K, :] = gfull[k].reshape(K, M)
        pbuf[...] = nn(pod_factor(gram[0:K, 0:K], aug_p, cinv), gram[0:K, :])
        pod_sweep(False, gram, pbuf, aug_p, cinv)

    @pl.when(c == 1)
    def _():
        inverse_block(2 * BLOCK, amat, ymat, aug, linv)

    for d in z_order:
        third[d][1].wait_recv()
    total = zw[0]
    for k in range(1, NZ):
        total = total + zw[k]
    wfull[pl.ds(z, 1)] = total[None]
    fifth = {}
    for d in z_order:
        fifth[d] = send(wfull.at[z], wfull.at[z], s_wz.at[d], r_wz.at[d], z_peers[d])
        sent.append(fifth[d])

    @pl.when(c == 0)
    def _():
        pod_sweep(False, gram, pbuf, aug_p, cinv)
        pod_sweep(True, gram, pbuf, aug_p, cinv)
        give_p.start()

    @pl.when(c == 1)
    def _():
        inverse_block(3 * BLOCK, amat, ymat, aug, linv)
        give_y.start()
        give_p.wait_recv()

    for d in z_order:
        fifth[d].wait_recv()
    p = pbuf[...]
    mine = mall.at[c, x]
    mall[pl.ds(c, 1), pl.ds(x, 1)] = nn(p, wfull[...].reshape(M, 128))[None, None]
    swaps = [send(mine, mine, s_mc.at[0], r_mc.at[0], partner)]
    moves = {}
    for d in (2, 1, 3):
        moves[d] = send(mine, mine, s_mx.at[d], r_mx.at[d], x_peers[d])
    for d in (1, 3, 2):
        moves[d].wait_recv()
        src = mall.at[c, lax.rem(x + NX - d, NX)]
        swaps.append(send(src, src, s_mc.at[d], r_mc.at[d], partner))
    for copy in swaps:
        copy.wait_recv()
    sent += swaps + list(moves.values())
    coeffs = jnp.concatenate([mall[k // NX, k % NX] for k in range(2 * NX)], axis=1)
    part = stacked(nt, coeffs, [f_ref[0], f_ref[1], f_ref[2]])
    half[...] = jnp.concatenate([part[:, 0:256], part[:, 256:]], axis=0).reshape(half.shape)
    rows = half.at[c]
    ry[pl.ds(y, 1)] = half[pl.ds(c, 1)]
    trade = {}
    for d in (2, 1, 3):
        trade[d] = send(rows, ry.at[y], s_y.at[d], r_y.at[d], y_peers[d])
    mc_out[...] = coeffs

    width = pod_out.shape[0]
    shift = lax.rem(NY - y, NY) * K
    picked = pltpu.roll(pbuf[pl.ds(pl.multiple_of(y * width, width), width), :] * scale, shift, 1)
    cuts = [picked[:, K * d : K * d + K] for d in slots]
    picked = jnp.concatenate([cuts[e // 2] for e in range(2 * NY)], axis=1)
    outer = nn(jnp.concatenate(split(picked), axis=0), parts_ref[...], None)
    pod_out[...] = outer[0:width] + outer[width:]

    for d in (1, 3, 2):
        trade[d].wait_recv()
    rfull[pl.ds(c, 1)] = (((ry[0] + ry[1]) + ry[2]) + ry[3])[None]
    last = send(rfull.at[c], rfull.at[c], s_p.at[0], r_p.at[0], partner)

    @pl.when(c == 0)
    def _():
        give_y.wait_recv()

    last.wait_recv()
    sent += list(trade.values()) + [last]
    right = jnp.concatenate([rfull[0], rfull[1]], axis=1)
    surrogate = nn(nt(right, ymat[...]), ymat[...])
    fit_out[...] = stacked(nn, surrogate, [f_ref[0], f_ref[1], f_ref[2]])
    chaos_out[...] = chaos_scale * surrogate[:, 0 : chaos_out.shape[1]]

    @pl.when(c == 0)
    def _():
        give_p.wait_send()

    @pl.when(c == 1)
    def _():
        give_y.wait_send()

    for copy in sent:
        copy.wait_send()


def main(own, samples, rates_t, order, powers, terms, scale, chaos_scale):
    f32, bf16 = jnp.float32, jnp.bfloat16
    dma = pltpu.SemaphoreType.DMA
    cells, width = samples.shape
    anywhere = pl.BlockSpec(memory_space=pl.ANY)
    square = pltpu.VMEM((TERM_PAD, TERM_PAD), f32)
    return pl.pallas_call(
        functools.partial(main_kernel, scale, chaos_scale),
        out_shape=(
            jax.ShapeDtypeStruct((K, width), f32),
            jax.ShapeDtypeStruct((K, width), f32),
            jax.ShapeDtypeStruct((K, terms), f32),
            jax.ShapeDtypeStruct((K // NY, cells), f32),
        ),
        in_specs=[anywhere] * 2 + [VMEM] * 4,
        out_specs=(VMEM,) * 4,
        scratch_shapes=[
            pltpu.VMEM((NY, K, cells), f32),
            pltpu.VMEM((cells, width), bf16),
            pltpu.VMEM((2 * M, cells), bf16),
            pltpu.VMEM((2 * M, width), f32),
            pltpu.VMEM((2 * K, 2 * M), f32),
            pltpu.VMEM((M, width), f32),
            pltpu.VMEM((2, NX, 8, M), f32),
            square,
            square,
            pltpu.VMEM((8, TERM_PAD), jnp.int32),
            pltpu.VMEM((TERM_PAD, TABLE), bf16),
            pltpu.VMEM((TERM_PAD, TABLE), bf16),
            pltpu.VMEM((TABLE, CHUNK), bf16),
            pltpu.VMEM((TABLE, CHUNK), bf16),
            pltpu.VMEM((PART, CHUNK), f32),
            pltpu.VMEM((NX, M, 128), f32),
            pltpu.VMEM((NX, 8, M), f32),
            pltpu.VMEM((NX, M, 128), f32),
            pltpu.VMEM((NX, 8, M), f32),
            pltpu.VMEM((NX, M, 128), f32),
            pltpu.VMEM((NX, 8, M), f32),
            pltpu.VMEM((NZ, M // NZ, 128), f32),
            pltpu.VMEM((NZ, M // NZ, 128), f32),
            pltpu.VMEM((NZ, 8, M), f32),
            pltpu.VMEM((NZ, M // NZ, 128), f32),
            pltpu.VMEM((NX, 8, M), f32),
            pltpu.VMEM((NY, 2, NX, 8, M), f32),
            square,
            *ELIMINATION,
            pltpu.VMEM((M, M), f32),
            pltpu.VMEM((K, 2 * K), f32),
            pltpu.VMEM((K, K), f32),
            pltpu.VMEM((K, M), f32),
            pltpu.VMEM((3, TERM_PAD, width), bf16),
            pltpu.VMEM((2, NX, K, 128), f32),
            pltpu.VMEM((2, K, 256), f32),
            pltpu.VMEM((NY, K, 256), f32),
            pltpu.VMEM((2, K, 256), f32),
            dma((NY, 2 * PIECES)), dma((NY, 2 * PIECES)), dma((1,)), dma((1,)),
            dma((NX,)), dma((NX,)),
            dma((2, NX)), dma((2, NX)),
            dma((2, NZ)), dma((2, NZ)),
            dma((NZ,)), dma((NZ,)),
            dma((NX,)), dma((NX,)),
            dma((NY,)), dma((NY,)),
            dma((NY,)), dma((NY,)),
            dma((2,)), dma((2,)),
            dma((NX,)), dma((NX,)),
            dma((NX,)), dma((NX,)),
            dma((NY,)), dma((NY,)),
            dma((1,)), dma((1,)),
            dma((2,)),
        ],
        compiler_params=pltpu.CompilerParams(
            collective_id=0, has_side_effects=True, vmem_limit_bytes=60 * 2**20
        ),
        cost_estimate=cost(10**11, 2 * 10**7),
    )(own, samples, rates_t, order, powers, table_codes())


def hand_over_kernel(*refs):
    count = len(refs) // 2
    for src, dst in zip(refs[:count], refs[count:]):
        dst[...] = src[...]


def hand_over(arrays):
    return pl.pallas_call(
        hand_over_kernel,
        out_shape=tuple(jax.ShapeDtypeStruct(a.shape, a.dtype) for a in arrays),
        in_specs=[VMEM] * len(arrays),
        out_specs=(VMEM,) * len(arrays),
    )(*arrays)


def local(snapshots, samples, sample_rates, sample_order, term_powers):
    total, terms = sample_rates.shape[0], term_powers.shape[0]
    cell_count = snapshots.shape[0] * lax.axis_size("space")
    outs = main(
        snapshots.T, samples, sample_rates.T, sample_order[None], term_powers.T,
        terms, math.sqrt(cell_count), math.sqrt(total),
    )
    coeffs, fitted, chaos, pod_modes = hand_over(outs)
    return (pod_modes.T, coeffs.T, fitted.T, chaos.T)


def solution(mesh):
    placed = (P("space", "col"), P("space", "col"), P(), P("col"), P())
    return jax.shard_map(
        local,
        mesh=mesh,
        in_specs=placed,
        out_specs=(P("space", "col"), P("col", None), P("col", None), P()),
        check_vma=False,
    )
```

```python
import functools
import itertools
import math

import jax
import jax.numpy as jnp
import numpy as np
from jax import lax
from jax.experimental import pallas as pl
from jax.experimental.pallas import tpu as pltpu
from jax.sharding import PartitionSpec as P

K = 64
M = 256
SWEEPS = 3
NX, NZ, NY = 4, 8, 4

top_degree = 4
ridge = 0.05

EXACT = lax.Precision.HIGHEST
TERM_PAD = 512
TABLE = 256
PART = 80
CHUNK = 1024
PIECES = 8
BLOCK = 128
MESH = pl.DeviceIdType.MESH
VMEM = pl.BlockSpec(memory_space=pltpu.VMEM)


def nn(a, b, precision=EXACT):
    return lax.dot_general(
        a, b, (((1,), (0,)), ((), ())), precision=precision, preferred_element_type=jnp.float32
    )


def nt(a, b, precision=EXACT):
    return lax.dot_general(
        a, b, (((1,), (1,)), ((), ())), precision=precision, preferred_element_type=jnp.float32
    )


def tn(a, b, precision=EXACT):
    return lax.dot_general(
        a, b, (((0,), (0,)), ((), ())), precision=precision, preferred_element_type=jnp.float32
    )


def cost(flops, bytes_accessed):
    return pl.CostEstimate(flops=flops, bytes_accessed=bytes_accessed, transcendentals=0)


def eye(n):
    rows = lax.broadcasted_iota(jnp.int32, (n, n), 0)
    return (rows == lax.broadcasted_iota(jnp.int32, (n, n), 1)).astype(jnp.float32)


def pivot_block(top, at, w):
    r = [jnp.broadcast_to(top[k : k + 1, :], (8, w)) for k in range(8)]
    a = [
        [jnp.broadcast_to(r[i][:, at + j : at + j + 1], (8, w)) for j in range(i + 1)] for i in range(8)
    ]
    s = [[None] * 8 for _ in range(8)]
    inv = [None] * 8
    for j in range(8):
        inv[j] = lax.rsqrt(a[j][j])
        r[j] = r[j] * inv[j]
        for i in range(j + 1, 8):
            s[i][j] = a[i][j] * inv[j]
        for i in range(j + 1, 8):
            for k in range(j + 1, i + 1):
                a[i][k] = a[i][k] - s[i][j] * s[k][j]
            r[i] = r[i] - s[i][j] * r[j]
    q = [None] * 8
    for k in reversed(range(8)):
        v = r[k]
        for m in reversed(range(k + 1, 8)):
            v = v - s[m][k] * q[m]
        q[k] = v * inv[k]
    return r, q


def merge_rows(r, w):
    sub = lax.broadcasted_iota(jnp.int32, (8, w), 0)
    rows = r[0]
    for k in range(1, 8):
        rows = jnp.where(sub == k, r[k], rows)
    return rows


def inverse_factor(aug, out, n):
    w = 2 * n
    groups = n // 8

    def body(b, carry):
        r, q = pivot_block(aug[0:8, :], 0, w)
        out[pl.ds(pl.multiple_of(8 * b, 8), 8), :] = pltpu.roll(merge_rows(r, w), 8 * b + n, 1)[:, :n]
        rest = aug[8:n, :].reshape(groups - 1, 8, w)
        upd = rest
        for k in reversed(range(8)):
            upd = upd - jnp.broadcast_to(rest[:, :, k : k + 1], rest.shape) * q[k][None]
        aug[0 : n - 8, :] = pltpu.roll(upd.reshape(n - 8, w), w - 8, 1)
        return carry

    lax.fori_loop(0, groups, body, 0)


def pivot_values(top, at):
    r = [[jnp.broadcast_to(piece[k : k + 1, :], (8, 128)) for piece in top] for k in range(8)]
    a = [
        [jnp.broadcast_to(r[i][0][:, at + j : at + j + 1], (8, 128)) for j in range(i + 1)]
        for i in range(8)
    ]
    low = [[None] * 8 for _ in range(8)]
    q = [None] * 8
    for j in range(8):
        inv = lax.rsqrt(a[j][j])
        r[j] = [v * inv for v in r[j]]
        for k in range(j):
            low[j][k] = low[j][k] * inv
        low[j][j] = inv
        for k in range(j + 1):
            term = [low[j][k] * v for v in r[j]]
            q[k] = term if k == j else [u + v for u, v in zip(q[k], term)]
        s = {i: a[i][j] * inv for i in range(j + 1, 8)}
        for i in range(j + 1, 8):
            for k in range(j + 1, i + 1):
                a[i][k] = a[i][k] - s[i] * s[k]
        for i in range(j + 1, 8):
            r[i] = [u - s[i] * v for u, v in zip(r[i], r[j])]
            for k in range(j + 1):
                step = s[i] * low[j][k]
                low[i][k] = -step if low[i][k] is None else low[i][k] - step
    return r, q


def merge_values(r):
    sub = lax.broadcasted_iota(jnp.int32, (8, 128), 0)
    pieces = []
    for p in range(len(r[0])):
        rows = r[0][p]
        for k in range(1, 8):
            rows = jnp.where(sub == k, r[k][p], rows)
        pieces.append(rows)
    return jnp.concatenate(pieces, axis=1) if len(pieces) > 1 else pieces[0]


def pod_factor(m, aug, cinv):
    full = jnp.concatenate([m, eye(K)], axis=1)
    rows = [full[8 * i : 8 * i + 8, :] for i in range(K // 8)]
    for b in range(K // 8):
        r, q = pivot_values([rows[b]], 8 * b)
        cinv[8 * b : 8 * b + 8, :] = merge_values(r)[:, K:]
        for i in range(b + 1, K // 8):
            v = rows[i]
            for k in reversed(range(8)):
                at = 8 * b + k
                v = v - jnp.broadcast_to(rows[i][:, at : at + 1], (8, 128)) * q[k][0]
            rows[i] = v
    return cinv[...]


def pod_sweep(last, gram, zbuf, aug, cinv):
    z = zbuf[...]
    w = nn(z, gram[...])
    c = pod_factor(nt(z, w), aug, cinv)
    zbuf[...] = nn(c, z if last else w)


def combos():
    return [c for c in itertools.product(range(top_degree + 1), repeat=4) if sum(c) <= top_degree]


def table_codes():
    column = np.full((TABLE, 1), -1, np.int32)
    for m, c in enumerate(combos()):
        for part in range(3):
            column[PART * part + m] = sum(e * 5**i for i, e in enumerate(c))
    return jnp.asarray(column)


def selector(powers, codes):
    code = powers[0:1, :]
    for i in range(1, 4):
        code = code + powers[i : i + 1, :] * 5**i
    return jnp.where(codes == code, 1.0, 0.0).T.astype(jnp.bfloat16)


def fill_table(levels, first, parts, table):
    for m, c in enumerate(combos()):
        row = None
        for i, e in enumerate(c):
            if e:
                level = levels[e][first + i : first + i + 1, :]
                row = level if row is None else row * level
        table[m : m + 1, :] = jnp.ones_like(levels[1][0:1, :]) if row is None else row
    full = table[...]
    high = full.astype(jnp.bfloat16)
    left = full - high.astype(jnp.float32)
    mid = left.astype(jnp.bfloat16)
    parts[0:PART, :] = high
    parts[PART : 2 * PART, :] = mid
    parts[2 * PART : 3 * PART, :] = (left - mid.astype(jnp.float32)).astype(jnp.bfloat16)


def features(points, sa, sb, ta, tb, table):
    he = [jnp.ones_like(points), points]
    for d in range(1, top_degree):
        he.append(points * he[d] - d * he[d - 1])
    levels = [he[d] / math.sqrt(math.factorial(d)) for d in range(top_degree + 1)]
    fill_table(levels, 0, ta, table)
    fill_table(levels, 4, tb, table)
    return nn(sa[...], ta[...], None) * nn(sb[...], tb[...], None)


def picked_points(rates, order):
    total, width = rates.shape[1], order.shape[1]
    high = rates.astype(jnp.bfloat16).astype(jnp.float32)
    left = rates - high
    mid = left.astype(jnp.bfloat16).astype(jnp.float32)
    parts = jnp.concatenate([high, mid, left - mid, jnp.zeros_like(left)], axis=0).astype(jnp.bfloat16)
    piece = 512
    row = lax.broadcasted_iota(jnp.int32, (piece, width), 0)
    found = jnp.zeros((32, width), jnp.float32)
    for at in range(0, total, piece):
        hit = jnp.where(row == order - at, 1.0, 0.0).astype(jnp.bfloat16)
        found = found + nn(parts[:, at : at + piece], hit, None)
    return (found[0:8] + found[8:16]) + found[16:24]


def inverse_block(lo, amat, ymat, aug, linv):
    hi = lo + BLOCK
    aug[...] = jnp.concatenate([amat[lo:hi, lo:hi], eye(BLOCK)], axis=1)
    inverse_factor(aug, linv, BLOCK)
    li = linv[...]
    if lo:
        ymat[lo:hi, 0:lo] = nn(li, ymat[lo:hi, 0:lo])
    ymat[lo:hi, lo:hi] = li
    if hi < TERM_PAD:
        panel = nt(amat[hi:, lo:hi], li)
        amat[hi:, hi:] = amat[hi:, hi:] - nt(panel, panel)
        ymat[hi:, 0:hi] = ymat[hi:, 0:hi] - nn(panel, ymat[lo:hi, 0:hi])


ELIMINATION = [
    pltpu.VMEM((BLOCK, 2 * BLOCK), jnp.float32),
    pltpu.VMEM((BLOCK, BLOCK), jnp.float32),
]


def split(x):
    high = x.astype(jnp.bfloat16)
    return high, (x - high.astype(jnp.float32)).astype(jnp.bfloat16)


def thirds(x):
    high = x.astype(jnp.bfloat16)
    left = x - high.astype(jnp.float32)
    mid = left.astype(jnp.bfloat16)
    return high, mid, (left - mid.astype(jnp.float32)).astype(jnp.bfloat16)


def stacked(dot, x, parts):
    n = x.shape[0]
    high, mid, low = thirds(x)
    a = dot(jnp.concatenate([high, mid, low], axis=0), parts[0], None)
    b = dot(jnp.concatenate([high, mid], axis=0), parts[1], None)
    c = dot(high, parts[2], None)
    return a[0:n] + ((a[n : 2 * n] + b[0:n]) + ((a[2 * n :] + b[n:]) + c))


def gram_product(first, piece, slots, shards, parts_ref, gacc):
    both = jnp.concatenate([half for e in range(NY) for half in split(shards[slots[e], :, piece])], axis=0)
    parts_ref[:, piece] = both
    gram = nt(both[0 : 2 * K], both, None)
    gacc[...] = gram if first else gacc[...] + gram


def sample_product(first, piece, samples_ref, parts_ref, acc):
    out = nn(parts_ref[:, piece], samples_ref[piece, :], None)
    acc[...] = out if first else acc[...] + out


def place():
    s = lax.axis_index("space")
    return s // (NZ * 2), (s // 2) % NZ, s % 2, lax.axis_index("col")


def device(x, z, c, y):
    return {"space": (x * NZ + z) * 2 + c, "col": y}


def send(src, dst, send_sem, recv_sem, peer):
    copy = pltpu.make_async_remote_copy(
        src_ref=src,
        dst_ref=dst,
        send_sem=send_sem,
        recv_sem=recv_sem,
        device_id=peer,
        device_id_type=MESH,
    )
    copy.start()
    return copy


def lanes(k):
    return pl.ds(pl.multiple_of(k * 128, 128), 128)


def main_kernel(
    scale, chaos_scale,
    own_hbm, samples_hbm, rates_ref, order_ref, powers_ref, codes_ref,
    mc_out, fit_out, chaos_out, pod_out,
    shards, samples_ref, parts_ref, acc, gacc, w_ref, g_ref,
    hh, hl, powers, sa, sb, ta, tb, table,
    cw, cg, sxw, sxg, rxw, rxg, xw, zw, zg, wfull, gx, gfull,
    ymat, aug, linv, gram, aug_p, cinv, pbuf, f_ref, y_parts,
    mall, half, ry, rfull,
    s_ag, r_ag, s_gp, r_gp,
    s_c, r_c, s_x, r_x, s_z, r_z, s_wz, r_wz, s_gx, r_gx, s_gy, r_gy, s_gc, r_gc,
    s_swap, r_swap, s_mx, r_mx, s_mc, r_mc, s_y, r_y, s_p, r_p, load,
):
    x, z, c, y = place()
    xs = [lax.rem(x + d, NX) for d in range(NX)]
    zs = [lax.rem(z + d, NZ) for d in range(NZ)]
    ys = [lax.rem(y + d, NY) for d in range(NY)]
    partner = device(x, z, 1 - c, y)
    x_peers = [device(xs[d], z, c, y) for d in range(NX)]
    z_peers = [device(x, zs[d], c, y) for d in range(NZ)]
    y_peers = [device(x, z, c, ys[d]) for d in range(NY)]
    x_order, z_order, y_order = (2, 1, 3, 0), (4, 3, 5, 2, 6, 1, 7), (2, 1, 3)
    loads = [
        pltpu.make_async_copy(own_hbm, shards.at[0], load.at[0]),
        pltpu.make_async_copy(samples_hbm, samples_ref, load.at[1]),
    ]
    for copy in loads:
        copy.start()
    peers = y_peers[1:] + [partner] + x_peers[1:] + z_peers[1:]
    barrier = pltpu.get_barrier_semaphore()
    for peer in peers:
        pl.semaphore_signal(barrier, inc=1, device_id=peer, device_id_type=MESH)
    for ref in (hh, hl, ymat, ta, tb, table):
        ref[...] = jnp.zeros_like(ref)
    powers[...] = jnp.full_like(powers, -1)
    powers[:, 0 : powers_ref.shape[1]] = powers_ref[...]
    pl.semaphore_wait(barrier, len(peers))
    sent = []

    top, bottom = pl.ds(0, K // 2), pl.ds(K // 2, K // 2)
    cells = samples_ref.shape[0]
    pieces = [pl.ds(at, cells // PIECES) for at in range(0, cells, cells // PIECES)]
    near = {}
    for i, piece in enumerate(pieces):
        for d in (3, 1):
            slot = NY - d
            near[d, i] = send(
                own_hbm.at[:, piece], shards.at[slot, :, piece], s_ag.at[d, i], r_ag.at[slot, i], y_peers[d]
            )
            sent.append(near[d, i])
    far = {}

    def relay(i):
        for h, (d, src, part) in enumerate(((3, 1, top), (1, 3, bottom))):
            near[d, i].wait_recv()
            far[h, i] = send(
                shards.at[src, part, pieces[i]], shards.at[2, part, pieces[i]],
                s_ag.at[2 * h, PIECES + i], r_ag.at[2 * h, PIECES + i], y_peers[d],
            )
            sent.append(far[h, i])

    sa[...] = selector(powers[0:4, :], codes_ref[...])
    sb[...] = selector(powers[4:8, :], codes_ref[...])
    total = rates_ref.shape[1]

    def chunk(step, carry):
        v = rates_ref[:, pl.ds(pl.multiple_of(step * CHUNK, CHUNK), CHUNK)]
        high, low = split(features(v, sa, sb, ta, tb, table))
        hh[...] += nt(high, high, None)
        hl[...] += nt(high, low, None)
        return carry

    lax.fori_loop(0, total // CHUNK, chunk, 0)
    for i in range(4):
        relay(i)
    f_high, f_mid, f_low = thirds(
        features(picked_points(rates_ref[...], order_ref[...]), sa, sb, ta, tb, table)
    )
    f_ref[0] = f_high
    f_ref[1] = f_mid
    f_ref[2] = f_low
    amat = hh
    amat[...] = hh[...] + hl[...] + hl[...].T + (ridge * total) * eye(TERM_PAD)
    inverse_block(0, amat, ymat, aug, linv)
    relay(4)
    relay(5)
    inverse_block(BLOCK, amat, ymat, aug, linv)
    relay(6)
    relay(7)

    for copy in loads:
        copy.wait()
    slots = (0, 1, 3, 2)
    for i, piece in enumerate(pieces):
        far[0, i].wait_recv()
        far[1, i].wait_recv()
        gram_product(i == 0, piece, slots, shards, parts_ref, gacc)
        if i < PIECES - 1:
            sample_product(i == 0, piece, samples_ref, parts_ref, acc)
    grams = gacc[0:K, :] + gacc[K:, :]
    blocks = [grams[:, 2 * K * e : 2 * K * e + K] + grams[:, 2 * K * e + K : 2 * K * (e + 1)] for e in (0, 1, 3, 2)]
    g_ref[...] = pltpu.roll(jnp.concatenate(blocks, axis=1), y * K, 1).reshape(g_ref.shape)
    early = send(g_ref.at[1 - c], cg, s_gp.at[0], r_gp.at[0], partner)
    sent.append(early)

    sample_product(False, pieces[-1], samples_ref, parts_ref, acc)
    early.wait_recv()
    second = {}
    for d in x_order:
        gsum = g_ref[c, xs[d]] + cg[xs[d]]
        if d:
            sxg[d] = gsum
            second[d] = [send(sxg.at[d], rxg.at[x], s_x.at[0, d], r_x.at[0, d], x_peers[d])]
        else:
            rxg[pl.ds(x, 1)] = gsum[None]
    for e in range(NY):
        row = pl.multiple_of(ys[slots[e]] * K, K)
        lo = 2 * K * e
        w_ref[pl.ds(row, K), :] = acc[lo : lo + K, :] + acc[lo + K : lo + 2 * K, :]

    first = {}
    for d in x_order:
        other = (1 - c) * NX + xs[d]
        first[d] = send(w_ref.at[:, lanes(other)], cw.at[d], s_c.at[d], r_c.at[d], partner)
        sent.append(first[d])
    for d in x_order:
        first[d].wait_recv()
        wsum = w_ref[:, lanes(c * NX + xs[d])] + cw[d]
        if d:
            sxw[d] = wsum
            second[d].append(send(sxw.at[d], rxw.at[x], s_x.at[1, d], r_x.at[1, d], x_peers[d]))
            sent += second[d]
        else:
            rxw[pl.ds(x, 1)] = wsum[None]

    for d in (1, 3, 2):
        second[d][0].wait_recv()
    sxg[0] = ((rxg[0] + rxg[1]) + rxg[2]) + rxg[3]
    zg[pl.ds(z, 1)] = sxg[0][None]
    third = {}
    for d in z_order:
        third[d] = [send(sxg.at[0], zg.at[z], s_z.at[0, d], r_z.at[0, d], z_peers[d])]
    for d in z_order:
        third[d][0].wait_recv()
    total = zg[0]
    for k in range(1, NZ):
        total = total + zg[k]
    gx[pl.ds(x, 1)] = total[None]
    fourth = {}
    for d in (2, 1, 3):
        fourth[d] = send(gx.at[x], gx.at[x], s_gx.at[d], r_gx.at[d], x_peers[d])
        sent.append(fourth[d])

    for d in (1, 3, 2):
        second[d][1].wait_recv()
    xw[...] = (((rxw[0] + rxw[1]) + rxw[2]) + rxw[3]).reshape(xw.shape)
    for d in z_order:
        third[d].append(send(xw.at[zs[d]], zw.at[z], s_z.at[1, d], r_z.at[1, d], z_peers[d]))
        sent += third[d]
    zw[pl.ds(z, 1)] = xw[pl.ds(z, 1)]

    for d in (1, 3, 2):
        fourth[d].wait_recv()
    gfull[pl.ds(y, 1), pl.ds(c, 1)] = gx[...][None, None]
    sixth = {}
    for d in y_order:
        sixth[d] = send(gx, gfull.at[y, c], s_gy.at[d], r_gy.at[d], y_peers[d])
        sent.append(sixth[d])
    seventh = [send(gx, gfull.at[y, c], s_gc.at[0], r_gc.at[0], partner)]
    for d in (1, 3, 2):
        sixth[d].wait_recv()
        src = lax.rem(y + NY - d, NY)
        seventh.append(send(gfull.at[src, c], gfull.at[src, c], s_gc.at[d], r_gc.at[d], partner))
    sent += seventh
    for copy in seventh:
        copy.wait_recv()

    tail = pl.ds(TERM_PAD - 2 * BLOCK, 2 * BLOCK)
    give_p = pltpu.make_async_remote_copy(
        src_ref=pbuf, dst_ref=pbuf, send_sem=s_swap.at[0], recv_sem=r_swap.at[0],
        device_id=partner, device_id_type=MESH,
    )
    give_y = pltpu.make_async_remote_copy(
        src_ref=ymat.at[tail, :], dst_ref=ymat.at[tail, :], send_sem=s_swap.at[1], recv_sem=r_swap.at[1],
        device_id=partner, device_id_type=MESH,
    )

    @pl.when(c == 0)
    def _():
        for k in range(NY):
            gram[K * k : K * k + K, :] = gfull[k].reshape(K, M)
        pbuf[...] = nn(pod_factor(gram[0:K, 0:K], aug_p, cinv), gram[0:K, :])
        pod_sweep(False, gram, pbuf, aug_p, cinv)

    @pl.when(c == 1)
    def _():
        inverse_block(2 * BLOCK, amat, ymat, aug, linv)

    for d in z_order:
        third[d][1].wait_recv()
    total = zw[0]
    for k in range(1, NZ):
        total = total + zw[k]
    wfull[pl.ds(z, 1)] = total[None]
    fifth = {}
    for d in z_order:
        fifth[d] = send(wfull.at[z], wfull.at[z], s_wz.at[d], r_wz.at[d], z_peers[d])
        sent.append(fifth[d])

    @pl.when(c == 0)
    def _():
        pod_sweep(False, gram, pbuf, aug_p, cinv)
        pod_sweep(True, gram, pbuf, aug_p, cinv)
        give_p.start()

    @pl.when(c == 1)
    def _():
        inverse_block(3 * BLOCK, amat, ymat, aug, linv)
        give_y.start()
        give_p.wait_recv()

    for d in z_order:
        fifth[d].wait_recv()
    p = pbuf[...]
    mine = mall.at[c, x]
    mall[pl.ds(c, 1), pl.ds(x, 1)] = nn(p, wfull[...].reshape(M, 128))[None, None]
    swaps = [send(mine, mine, s_mc.at[0], r_mc.at[0], partner)]
    moves = {}
    for d in (2, 1, 3):
        moves[d] = send(mine, mine, s_mx.at[d], r_mx.at[d], x_peers[d])
    for d in (1, 3, 2):
        moves[d].wait_recv()
        src = mall.at[c, lax.rem(x + NX - d, NX)]
        swaps.append(send(src, src, s_mc.at[d], r_mc.at[d], partner))
    for copy in swaps:
        copy.wait_recv()
    sent += swaps + list(moves.values())
    coeffs = jnp.concatenate([mall[k // NX, k % NX] for k in range(2 * NX)], axis=1)
    part = stacked(nt, coeffs, [f_ref[0], f_ref[1], f_ref[2]])
    half[...] = jnp.concatenate([part[:, 0:256], part[:, 256:]], axis=0).reshape(half.shape)
    rows = half.at[c]
    ry[pl.ds(y, 1)] = half[pl.ds(c, 1)]
    trade = {}
    for d in (2, 1, 3):
        trade[d] = send(rows, ry.at[y], s_y.at[d], r_y.at[d], y_peers[d])
    mc_out[...] = coeffs

    width = pod_out.shape[0]
    shift = lax.rem(NY - y, NY) * K
    picked = pltpu.roll(pbuf[pl.ds(pl.multiple_of(y * width, width), width), :] * scale, shift, 1)
    cuts = [picked[:, K * d : K * d + K] for d in slots]
    picked = jnp.concatenate([cuts[e // 2] for e in range(2 * NY)], axis=1)
    outer = nn(jnp.concatenate(split(picked), axis=0), parts_ref[...], None)
    pod_out[...] = outer[0:width] + outer[width:]

    @pl.when(c == 0)
    def _():
        give_y.wait_recv()

    inverse_parts = thirds(ymat[...])
    for i in range(3):
        y_parts[i] = inverse_parts[i]

    for d in (1, 3, 2):
        trade[d].wait_recv()
    rfull[pl.ds(c, 1)] = (((ry[0] + ry[1]) + ry[2]) + ry[3])[None]
    last = send(rfull.at[c], rfull.at[c], s_p.at[0], r_p.at[0], partner)

    last.wait_recv()
    sent += list(trade.values()) + [last]
    right = jnp.concatenate([rfull[0], rfull[1]], axis=1)
    factor = [y_parts[i] for i in range(3)]
    surrogate = stacked(nn, stacked(nt, right, factor), factor)
    fit_out[...] = stacked(nn, surrogate, [f_ref[0], f_ref[1], f_ref[2]])
    chaos_out[...] = chaos_scale * surrogate[:, 0 : chaos_out.shape[1]]

    @pl.when(c == 0)
    def _():
        give_p.wait_send()

    @pl.when(c == 1)
    def _():
        give_y.wait_send()

    for copy in sent:
        copy.wait_send()


def main(own, samples, rates_t, order, powers, terms, scale, chaos_scale):
    f32, bf16 = jnp.float32, jnp.bfloat16
    dma = pltpu.SemaphoreType.DMA
    cells, width = samples.shape
    anywhere = pl.BlockSpec(memory_space=pl.ANY)
    square = pltpu.VMEM((TERM_PAD, TERM_PAD), f32)
    return pl.pallas_call(
        functools.partial(main_kernel, scale, chaos_scale),
        out_shape=(
            jax.ShapeDtypeStruct((K, width), f32),
            jax.ShapeDtypeStruct((K, width), f32),
            jax.ShapeDtypeStruct((K, terms), f32),
            jax.ShapeDtypeStruct((K // NY, cells), f32),
        ),
        in_specs=[anywhere] * 2 + [VMEM] * 4,
        out_specs=(VMEM,) * 4,
        scratch_shapes=[
            pltpu.VMEM((NY, K, cells), f32),
            pltpu.VMEM((cells, width), bf16),
            pltpu.VMEM((2 * M, cells), bf16),
            pltpu.VMEM((2 * M, width), f32),
            pltpu.VMEM((2 * K, 2 * M), f32),
            pltpu.VMEM((M, width), f32),
            pltpu.VMEM((2, NX, 8, M), f32),
            square,
            square,
            pltpu.VMEM((8, TERM_PAD), jnp.int32),
            pltpu.VMEM((TERM_PAD, TABLE), bf16),
            pltpu.VMEM((TERM_PAD, TABLE), bf16),
            pltpu.VMEM((TABLE, CHUNK), bf16),
            pltpu.VMEM((TABLE, CHUNK), bf16),
            pltpu.VMEM((PART, CHUNK), f32),
            pltpu.VMEM((NX, M, 128), f32),
            pltpu.VMEM((NX, 8, M), f32),
            pltpu.VMEM((NX, M, 128), f32),
            pltpu.VMEM((NX, 8, M), f32),
            pltpu.VMEM((NX, M, 128), f32),
            pltpu.VMEM((NX, 8, M), f32),
            pltpu.VMEM((NZ, M // NZ, 128), f32),
            pltpu.VMEM((NZ, M // NZ, 128), f32),
            pltpu.VMEM((NZ, 8, M), f32),
            pltpu.VMEM((NZ, M // NZ, 128), f32),
            pltpu.VMEM((NX, 8, M), f32),
            pltpu.VMEM((NY, 2, NX, 8, M), f32),
            square,
            *ELIMINATION,
            pltpu.VMEM((M, M), f32),
            pltpu.VMEM((K, 2 * K), f32),
            pltpu.VMEM((K, K), f32),
            pltpu.VMEM((K, M), f32),
            pltpu.VMEM((3, TERM_PAD, width), bf16),
            pltpu.VMEM((3, TERM_PAD, TERM_PAD), bf16),
            pltpu.VMEM((2, NX, K, 128), f32),
            pltpu.VMEM((2, K, 256), f32),
            pltpu.VMEM((NY, K, 256), f32),
            pltpu.VMEM((2, K, 256), f32),
            dma((NY, 2 * PIECES)), dma((NY, 2 * PIECES)), dma((1,)), dma((1,)),
            dma((NX,)), dma((NX,)),
            dma((2, NX)), dma((2, NX)),
            dma((2, NZ)), dma((2, NZ)),
            dma((NZ,)), dma((NZ,)),
            dma((NX,)), dma((NX,)),
            dma((NY,)), dma((NY,)),
            dma((NY,)), dma((NY,)),
            dma((2,)), dma((2,)),
            dma((NX,)), dma((NX,)),
            dma((NX,)), dma((NX,)),
            dma((NY,)), dma((NY,)),
            dma((1,)), dma((1,)),
            dma((2,)),
        ],
        compiler_params=pltpu.CompilerParams(
            collective_id=0, has_side_effects=True, vmem_limit_bytes=60 * 2**20
        ),
        cost_estimate=cost(10**11, 2 * 10**7),
    )(own, samples, rates_t, order, powers, table_codes())


def hand_over_kernel(*refs):
    count = len(refs) // 2
    for src, dst in zip(refs[:count], refs[count:]):
        dst[...] = src[...]


def hand_over(arrays):
    return pl.pallas_call(
        hand_over_kernel,
        out_shape=tuple(jax.ShapeDtypeStruct(a.shape, a.dtype) for a in arrays),
        in_specs=[VMEM] * len(arrays),
        out_specs=(VMEM,) * len(arrays),
    )(*arrays)


def local(snapshots, samples, sample_rates, sample_order, term_powers):
    total, terms = sample_rates.shape[0], term_powers.shape[0]
    cell_count = snapshots.shape[0] * lax.axis_size("space")
    outs = main(
        snapshots.T, samples, sample_rates.T, sample_order[None], term_powers.T,
        terms, math.sqrt(cell_count), math.sqrt(total),
    )
    coeffs, fitted, chaos, pod_modes = hand_over(outs)
    return (pod_modes.T, coeffs.T, fitted.T, chaos.T)


def solution(mesh):
    placed = (P("space", "col"), P("space", "col"), P(), P("col"), P())
    return jax.shard_map(
        local,
        mesh=mesh,
        in_specs=placed,
        out_specs=(P("space", "col"), P("col", None), P("col", None), P()),
        check_vma=False,
    )
```
